32 devices in a mesh: groups: 2 (over y), row: 4 (over z), col: 2 (over x), chan: 2 (over core).
Axes of the slice: x: 2, y: 2, z: 4, core: 2. Of those that a mesh axis runs over, the one named last changes fastest.
Arguments:
- layer_input: bfloat16 [2, 64, 32, 512], P(None, None, ('groups', 'col'), 'row'), parts along dimension 2, may hold values from -6 to 6
- features: bfloat16 [2, 64, 32, 512], P(None, 'chan', ('groups', 'col'), 'row'), parts along dimension 2, may hold values from -6 to 6
- vol_target: bfloat16 [8, 40, 32, 512], P('chan', None, ('groups', 'col'), 'row'), parts along dimension 2, may hold values from -6 to 6
- offsets: int32 [4, 4], P('row', ('groups', 'col')), parts along dimension 1, may hold values from 0 to 2, as said below
- w_first: bfloat16 [64, 64, 3, 3], replicated, may hold values from -0.25 to 0.25
- w_second: bfloat16 [64, 64, 3, 3], replicated, may hold values from -0.25 to 0.25
Outputs:
- grad_features: bfloat16 [2, 64, 32, 512], P(None, 'chan', ('groups', 'col'), 'row'), parts along dimension 2
- grad_w_first: float32 [128, 64, 3, 3], P('groups'), parts along dimension 0
- grad_w_second: float32 [128, 64, 3, 3], P('groups'), parts along dimension 0
The draws below stay inside these ranges and needn't reach their ends.
There are 2 independent parts, one for each index of `groups`. The reference program is written for one: setup_inputs(seed, part) draws one part's arguments, and reference() takes and returns one part's arrays. A program takes and returns all parts, laid end to end along the dimension named above; an argument that names none is the same for every part. Nothing has to cross between parts.
Inputs may be any that keep to these rules, and one draw needn't show every extreme that they name: `offsets`: each tile's entry is at most its own tile row index along the epipolar direction; tiles of the first row have 0, and some tile has exactly 2.
All inputs are finite; a program needn't handle non-finite values.
Results may differ from the reference program's by a relative error of at most 0.005.
Values may be sent and summed in bfloat16 or wider, within the bound.
No kernel may reach another device: no remote copies, remote signals or barrier semaphores. Data moves between devices by JAX's collectives and lax.ppermute only.
A program may use at most 64 MiB of HBM per device.

```python
import math
import jax
import jax.numpy as jnp
from jax import lax

CHANNELS = 64
GROUPS = 8
DISP = 40
MAXOFF = 2
BLOCK = 128
TILE_W = 8
NX = 16
NY = 512
TILES_Y = 4
TILES_X = 2


def draw_offsets(key, part):
    part_key = jax.random.fold_in(key, part)
    key_raw = jax.random.fold_in(part_key, 11)
    key_row = jax.random.fold_in(part_key, 12)
    key_col = jax.random.fold_in(part_key, 13)
    raw_values = jax.random.randint(key_raw, (TILES_Y, TILES_X), 0, MAXOFF + 1)
    tile_rows = lax.broadcasted_iota(jnp.int32, (TILES_Y, TILES_X), 0)
    tile_cols = lax.broadcasted_iota(jnp.int32, (TILES_Y, TILES_X), 1)
    bounded = jnp.minimum(raw_values, tile_rows)
    chosen_row = jax.random.randint(key_row, (), MAXOFF, TILES_Y)
    chosen_col = jax.random.randint(key_col, (), 0, TILES_X)
    picked = jnp.logical_and(tile_rows == chosen_row, tile_cols == chosen_col)
    return jnp.where(picked, MAXOFF, bounded).astype(jnp.int32)


def level_of(stream_key, dims, split, low, largest):
    loudness = 1.0
    for axis_at, blocks in split:
        draws = jax.random.uniform(jax.random.fold_in(jax.random.fold_in(stream_key, 6), axis_at), (blocks,), jnp.float32, low / len(split), largest / len(split))
        loudness = loudness * jnp.repeat(jnp.exp(draws), dims[axis_at] // blocks).reshape((-1,) + (1,) * (len(dims) - 1 - axis_at))
    return loudness


def centred(key, extent, spread, bound, shards=(), held_as=jnp.bfloat16):
    entries = spread * jax.random.normal(key, extent, jnp.float32)
    if shards:
        entries = entries * level_of(key, extent, shards, -0.22, 0.18)
    return jnp.clip(entries, -bound, bound).astype(held_as)


def setup_inputs(seed: int = 0, part: int = 0) -> dict:
    splits = jax.random.split(jax.random.key(seed), 7)
    part_keys = jax.random.split(jax.random.fold_in(splits[6], part), 7)
    return {
        "layer_input": centred(part_keys[0], (2, CHANNELS, NX, NY), 1.0, 6.0, ((2, 2), (3, 4))),
        "features": centred(part_keys[1], (2, CHANNELS, NX, NY), 1.0, 6.0, ((1, 2), (2, 2), (3, 4))),
        "vol_target": centred(part_keys[2], (GROUPS, DISP, NX, NY), 1.0, 6.0, ((0, 2), (2, 2), (3, 4))),
        "offsets": draw_offsets(jax.random.fold_in(jax.random.fold_in(splits[6], part), 71), part),
        "w_first": centred(splits[4], (CHANNELS, CHANNELS, 3, 3), (9 * CHANNELS) ** -0.5, 0.25),
        "w_second": centred(splits[5], (CHANNELS, CHANNELS, 3, 3), (9 * CHANNELS) ** -0.5, 0.25),
    }


def convolve(image, kernel):
    return lax.conv_general_dilated(image, kernel, (1, 1), 'SAME', precision=lax.Precision.HIGHEST)

def reference(layer_input, features, vol_target, offsets, w_first, w_second):
    group_size = CHANNELS // GROUPS
    input_f32 = layer_input.astype(jnp.float32)
    hidden = jnp.maximum(convolve(input_f32, w_first.astype(jnp.float32)), 0.0).astype(jnp.bfloat16)
    left_feat = features[0].astype(jnp.float32)
    right_feat = features[1].astype(jnp.float32)
    offset_map = jnp.repeat(jnp.repeat(offsets.T, TILE_W, axis=0), BLOCK, axis=1).astype(jnp.int32)
    padding = BLOCK * MAXOFF + DISP
    right_padded = jnp.pad(right_feat, ((0, 0), (0, 0), (padding, 0)))
    y_index = lax.broadcasted_iota(jnp.int32, (NX, NY), 1)
    columns = lax.broadcasted_iota(jnp.int32, (NX, NY), 0)

    def disparity_step(d, state_now):
        left_grad, right_grad = state_now
        source_rows = (y_index - d - BLOCK * offset_map + padding).astype(jnp.int32)
        shifted = right_padded[:, columns, source_rows]
        volume = (left_feat * shifted).reshape(GROUPS, group_size, NX, NY).sum(axis=1) / group_size
        target_plane = lax.dynamic_index_in_dim(vol_target, d, 1, keepdims=False).astype(jnp.float32)
        weighted = jnp.repeat(volume - target_plane, group_size, axis=0) / group_size
        left_grad = left_grad + weighted * shifted
        right_grad = right_grad.at[:, columns, source_rows].add(weighted * left_feat)
        return (left_grad, right_grad)
    initial = (jnp.zeros((CHANNELS, NX, NY), jnp.float32), jnp.zeros((CHANNELS, NX, NY + padding), jnp.float32))
    left_grad, right_grad = lax.fori_loop(0, DISP, disparity_step, initial)
    grad_features = jnp.stack([left_grad, right_grad[:, :, padding:]]).astype(jnp.bfloat16)
    grad_f32 = grad_features.astype(jnp.float32)
    _, pull_second = jax.vjp(convolve, hidden.astype(jnp.float32), w_second.astype(jnp.float32))
    hidden_pre, w2_sum = pull_second(grad_f32)
    hidden_grad = jnp.where(hidden > 0, hidden_pre, 0.0).astype(jnp.bfloat16)
    _, pull_first = jax.vjp(lambda kernel: convolve(input_f32, kernel), w_first.astype(jnp.float32))
    w1_sum, = pull_first(hidden_grad.astype(jnp.float32))
    factor = 1.0 / math.sqrt(2.0 * NX * NY)
    return (grad_features, w1_sum * factor, w2_sum * factor)
```

```python
import math

import jax
import jax.numpy as jnp
from jax import lax
from jax.experimental import pallas as pl
from jax.experimental.pallas import tpu as pltpu
from jax.sharding import PartitionSpec as P

DISP = 40
MAXOFF = 2


def passed_along(block, axis, distance):
    devices = range(lax.axis_size(axis))
    route = [(i - distance, i) for i in devices if i - distance in devices]
    return lax.ppermute(block, axis, route)


def extended(array, sides, width):
    for axis, dim in sides:
        peers, length = (lax.axis_size(axis), array.shape[dim])
        up = [(i, (i + 1) % peers) for i in range(peers - 1)]
        down = [(j, i) for i, j in up]
        last = lax.slice_in_dim(array, length - width, length, axis=dim)
        leading = lax.slice_in_dim(array, 0, width, axis=dim)
        before = lax.ppermute(last, axis, up)
        after = lax.ppermute(leading, axis, down)
        array = jnp.concatenate([before, array, after], axis=dim)
    return array


def correlation_kernel(offset_ref, left_ref, own_ref, one_ref, two_ref, three_ref, target_ref,
                       left_out, own_out, one_out, two_out, three_out):
    offset = offset_ref[0, 0]
    group_size, tile_w, block_rows = left_ref.shape
    inv_size = 1.0 / group_size
    shape = (tile_w, block_rows)
    lane = lax.broadcasted_iota(jnp.int32, shape, 1)
    left, main, spill = [], [], []
    for c in range(group_size):
        own, one, two, three = (r[c].astype(jnp.float32) for r in (own_ref, one_ref, two_ref, three_ref))
        left.append(left_ref[c].astype(jnp.float32))
        main.append(jnp.where(offset == 0, own, jnp.where(offset == 1, one, two)))
        spill.append(jnp.where(offset == 0, one, jnp.where(offset == 1, two, three)))
    zero = jnp.zeros(shape, jnp.float32)
    left_grad = [zero] * group_size
    whole_grad = [zero] * group_size
    spill_grad = [zero] * group_size
    for d in range(DISP):
        volume = None
        shifted = []
        for c in range(group_size):
            if d:
                moved = pltpu.roll(jnp.where(lane >= block_rows - d, spill[c], main[c]), d, 1)
            else:
                moved = main[c]
            shifted.append(moved)
            product = left[c] * moved
            volume = product if volume is None else volume + product
        weighted = (volume * inv_size - target_ref[0, d].astype(jnp.float32)) * inv_size
        for c in range(group_size):
            left_grad[c] = left_grad[c] + weighted * shifted[c]
            part = weighted * left[c]
            if d:
                part = pltpu.roll(part, block_rows - d, 1)
                spill_grad[c] = spill_grad[c] + jnp.where(lane >= block_rows - d, part, 0.0)
            whole_grad[c] = whole_grad[c] + part
    for c in range(group_size):
        main_grad = whole_grad[c] - spill_grad[c]
        left_out[c] = left_grad[c].astype(left_out.dtype)
        own_out[c] = jnp.where(offset == 0, main_grad, 0.0)
        one_out[c] = jnp.where(offset == 0, spill_grad[c], jnp.where(offset == 1, main_grad, 0.0)).astype(one_out.dtype)
        two_out[c] = jnp.where(offset == 1, spill_grad[c], jnp.where(offset == 2, main_grad, 0.0)).astype(two_out.dtype)
        three_out[c] = jnp.where(offset == 2, spill_grad[c], 0.0).astype(three_out.dtype)


def correlate(offset, left_feat, blocks, vol_target):
    local_ch, tile_w, block_rows = left_feat.shape
    groups = vol_target.shape[0]
    size = local_ch // groups
    tile = pl.BlockSpec((size, tile_w, block_rows), lambda g: (g, 0, 0))
    small = jax.ShapeDtypeStruct(left_feat.shape, jnp.bfloat16)
    return pl.pallas_call(
        correlation_kernel,
        grid=(groups,),
        in_specs=[pl.BlockSpec(memory_space=pltpu.SMEM)] + [tile] * 5
        + [pl.BlockSpec((1, DISP, tile_w, block_rows), lambda g: (g, 0, 0, 0))],
        out_specs=[tile] * 5,
        out_shape=[small, jax.ShapeDtypeStruct(left_feat.shape, jnp.float32), small, small, small],
        name="correlate",
    )(offset, left_feat, *blocks, vol_target)


def summed_over(partial, axis):
    peers = lax.axis_size(axis)
    step = 1
    while step < peers:
        rounded = partial.astype(jnp.bfloat16)
        arrived = lax.ppermute(rounded, axis, [(i, i ^ step) for i in range(peers)])
        partial = rounded.astype(jnp.float32) + arrived.astype(jnp.float32)
        step *= 2
    return partial


def body(layer_input, features, vol_target, offsets, w_first, w_second):
    all_channels = layer_input.shape[1]
    tile_w = layer_input.shape[2]
    block_rows = layer_input.shape[3]
    local_ch = features.shape[1]
    left_feat = features[0]
    right_feat = features[1]
    first_ch = lax.axis_index("chan") * local_ch
    blocks = [right_feat] + [passed_along(right_feat, "row", k) for k in range(1, MAXOFF + 2)]
    left_grad, own, *outgoing = correlate(offsets, left_feat, blocks, vol_target)
    right_grad = own
    for k, part in enumerate(outgoing, 1):
        right_grad = right_grad + passed_along(part, "row", -k).astype(jnp.float32)
    grad_features = jnp.stack([left_grad, right_grad.astype(jnp.bfloat16)])
    swap = [(i, i ^ 1) for i in range(2)]
    grad_maps = lax.all_gather(grad_features, "chan", axis=1, tiled=True)
    joined = extended(
        jnp.concatenate([layer_input, grad_maps], axis=1), (("row", 3), ("col", 2)), 1
    )
    input_halo = joined[:, :all_channels]
    grad_halo = joined[:, all_channels:]
    summed = None
    for a in range(3):
        for b in range(3):
            product = jnp.einsum(
                "oi,nixy->noxy",
                w_first[:, :, a, b],
                input_halo[:, :, a : a + tile_w, b : b + block_rows],
                preferred_element_type=jnp.float32,
            )
            summed = product if summed is None else summed + product
    hidden = jnp.maximum(summed, 0.0).astype(jnp.bfloat16)
    hidden_here = lax.dynamic_slice_in_dim(hidden, first_ch, local_ch, 1)
    own_halo = lax.dynamic_slice_in_dim(grad_halo, first_ch, local_ch, 1)
    second_pieces = []
    for a in range(3):
        for b in range(3):
            view = own_halo[:, :, 2 - a : 2 - a + tile_w, 2 - b : 2 - b + block_rows]
            second_pieces.append(
                jnp.einsum("noxy,nixy->oi", view, hidden, preferred_element_type=jnp.float32)
            )
    w2_cols = lax.dynamic_slice_in_dim(w_second, first_ch, local_ch, 1)
    summed = None
    for a in range(3):
        for b in range(3):
            view = grad_halo[:, :, 2 - a : 2 - a + tile_w, 2 - b : 2 - b + block_rows]
            product = jnp.einsum(
                "oi,noxy->nixy", w2_cols[:, :, a, b], view, preferred_element_type=jnp.float32
            )
            summed = product if summed is None else summed + product
    hidden_grad = jnp.where(hidden_here > 0, summed, 0.0).astype(jnp.bfloat16)
    first_pieces = []
    for a in range(3):
        for b in range(3):
            view = input_halo[:, :, a : a + tile_w, b : b + block_rows]
            first_pieces.append(
                jnp.einsum("noxy,nixy->oi", hidden_grad, view, preferred_element_type=jnp.float32)
            )
    partial = jnp.concatenate([jnp.stack(first_pieces), jnp.stack(second_pieces)], axis=2)
    for axis in ("col", "row"):
        partial = summed_over(partial, axis)
    factor = 1.0 / math.sqrt(
        2.0 * tile_w * lax.axis_size("col") * block_rows * lax.axis_size("row")
    )
    both = lax.all_gather(partial * factor, "chan", axis=1, tiled=True)
    both = both.reshape(3, 3, all_channels, 2 * all_channels).transpose(2, 3, 0, 1)
    return (grad_features, both[:, :all_channels], both[:, all_channels:])


def solution(mesh):
    return jax.shard_map(
        body,
        mesh=mesh,
        in_specs=(
            P(None, None, ("groups", "col"), "row"),
            P(None, "chan", ("groups", "col"), "row"),
            P("chan", None, ("groups", "col"), "row"),
            P("row", ("groups", "col")),
            P(),
            P(),
        ),
        out_specs=(
            P(None, "chan", ("groups", "col"), "row"),
            P("groups", None, None, None),
            P("groups", None, None, None),
        ),
        check_vma=False,
    )
```

```python
import functools
import math

import jax
import jax.numpy as jnp
from jax import lax
from jax.experimental import pallas as pl
from jax.experimental.pallas import tpu as pltpu
from jax.sharding import PartitionSpec as P

DISP = 40
MAXOFF = 2
F32 = jnp.float32
BF16 = jnp.bfloat16
SPACE = 12 << 20


def call(kernel, outs, *args, smem=0, scratch=(), flops=1 << 20, name=None):
    whole = pl.BlockSpec(memory_space=pltpu.VMEM)
    return pl.pallas_call(
        kernel,
        in_specs=[pl.BlockSpec(memory_space=pltpu.SMEM)] * smem + [whole] * (len(args) - smem),
        out_specs=[whole] * len(outs),
        out_shape=[jax.ShapeDtypeStruct(s, t) for s, t in outs],
        scratch_shapes=list(scratch),
        compiler_params=pltpu.CompilerParams(vmem_limit_bytes=SPACE),
        cost_estimate=pl.CostEstimate(flops=flops, bytes_accessed=1 << 20, transcendentals=0),
        name=name,
    )(*args)


def moved(block, axis, *distances):
    peers = lax.axis_size(axis)
    route = [(i - d, i) for d in distances for i in range(peers) if 0 <= i - d < peers]
    return lax.ppermute(block, axis, route)


def tap(rows, b, before, after):
    if b == 1:
        return rows
    lane = lax.broadcasted_iota(jnp.int32, rows.shape, 1)
    last = rows.shape[1] - 1
    if b == 0:
        return jnp.where(lane == 0, jnp.broadcast_to(before, rows.shape), pltpu.roll(rows, 1, 1))
    return jnp.where(lane == last, jnp.broadcast_to(after, rows.shape), pltpu.roll(rows, last, 1))


def nt(a, b):
    return lax.dot_general(a, b, (((1,), (1,)), ((), ())), preferred_element_type=F32)


def pack_kernel(layer_ref, features_ref, up_ref, down_ref):
    images, channels, tile_w, block_rows = layer_ref.shape
    local_ch = features_ref.shape[1]
    shape = (tile_w, block_rows)
    lane = lax.broadcasted_iota(jnp.int32, shape, 1)
    first = jnp.zeros(shape, F32)
    last = jnp.zeros(shape, F32)
    for n in range(images):
        for c in range(channels):
            tile = layer_ref[n, c].astype(F32)
            here = lane == n * channels + c
            first = jnp.where(here, jnp.broadcast_to(tile[:, :1], shape), first)
            last = jnp.where(here, jnp.broadcast_to(tile[:, block_rows - 1 :], shape), last)
    right = features_ref[1]
    up_ref[:local_ch] = right
    up_ref[local_ch] = last.astype(BF16)
    down_ref[:local_ch] = right
    down_ref[local_ch] = first.astype(BF16)


def correlation_kernel(merged, offset_ref, features_ref, one_ref, two_ref, three_ref, target_ref,
                       left_out, own_out, one_out, two_out, three_out, minus_out, moved_ref, residual_ref):
    offset = offset_ref[0, 0]
    row = lax.axis_index("row")
    local_ch, tile_w, block_rows = features_ref.shape[1:]
    groups = target_ref.shape[0]
    size = local_ch // groups
    inv_size = 1.0 / size
    shape = (tile_w, block_rows)
    lane = lax.broadcasted_iota(jnp.int32, shape, 1)
    zero = jnp.zeros(shape, F32)
    low_three = row <= MAXOFF

    def column(tile, at, kind, c, into):
        picked = jnp.broadcast_to(tile[:, at : at + 1], shape)
        return jnp.where(lane == kind * local_ch + c, picked, into)

    def one_group(g, edges):
        end_main, end_spill, start_main, end_left, start_left = edges
        base = g * size

        def scaled_left(c):
            return features_ref[0, base + c].astype(F32) * inv_size

        left, main, spill = [], [], []
        for c in range(size):
            own = features_ref[1, base + c].astype(F32)
            one, two, three = (r[base + c].astype(F32) for r in (one_ref, two_ref, three_ref))
            if merged:
                three = jnp.where(low_three, 0.0, three)
            left.append(scaled_left(c))
            main.append(jnp.where(offset == 0, own, jnp.where(offset == 1, one, two)))
            spill.append(jnp.where(offset == 0, one, jnp.where(offset == 1, two, three)))
        for d in range(DISP):
            products = []
            for c in range(size):
                moved = main[c]
                if d:
                    moved = pltpu.roll(jnp.where(lane >= block_rows - d, spill[c], moved), d, 1)
                moved_ref[d, c] = moved
                products.append(left[c] * moved)
            while len(products) > 1:
                products = [sum(products[i : i + 2]) for i in range(0, len(products), 2)]
            residual_ref[d] = products[0] - target_ref[g, d].astype(F32)
        for first in range(0, size, 2):
            channels = range(first, min(first + 2, size))
            left_grad = {c: zero for c in channels}
            whole_grad = {c: zero for c in channels}
            spill_grad = {c: zero for c in channels}
            scaled = {c: scaled_left(c) for c in channels}
            for d in range(DISP):
                residual = residual_ref[d]
                for c in channels:
                    left_grad[c] = left_grad[c] + residual * moved_ref[d, c]
                    part = residual * scaled[c]
                    if d:
                        part = pltpu.roll(part, block_rows - d, 1)
                        spill_grad[c] = spill_grad[c] + jnp.where(lane >= block_rows - d, part, 0.0)
                    whole_grad[c] = whole_grad[c] + part
            for c in channels:
                ch = base + c
                main_grad = whole_grad[c] - spill_grad[c]
                final = (left_grad[c] * inv_size).astype(BF16)
                left_out[ch] = final
                final = final.astype(F32)
                own_out[ch] = jnp.where(offset == 0, main_grad, 0.0)
                one_out[ch] = jnp.where(
                    offset == 0, spill_grad[c], jnp.where(offset == 1, main_grad, 0.0)
                ).astype(BF16)
                two_out[ch] = jnp.where(
                    offset == 1, spill_grad[c], jnp.where(offset == 2, main_grad, 0.0)
                ).astype(BF16)
                far = offset == 2
                if merged:
                    far = jnp.logical_and(far, jnp.logical_not(low_three))
                three_out[ch] = jnp.where(far, spill_grad[c], 0.0).astype(BF16)
                end_main = column(main_grad, block_rows - 1, 0, ch, end_main)
                end_spill = column(spill_grad[c], block_rows - 1, 0, ch, end_spill)
                start_main = column(main_grad, 0, 1, ch, start_main)
                end_left = column(final, block_rows - 1, 2, ch, end_left)
                start_left = column(final, 0, 3, ch, start_left)
        return end_main, end_spill, start_main, end_left, start_left

    end_main, end_spill, start_main, end_left, start_left = lax.fori_loop(
        0, groups, one_group, (zero,) * 5
    )

    def edges(k):
        tile = jnp.where(offset == k + 1, end_main, 0.0) + jnp.where(offset == k, end_spill, 0.0)
        tile = tile + jnp.where(offset == k - 1, start_main, 0.0)
        return tile + (end_left if k == -1 else start_left if k == 1 else 0.0)

    own_out[local_ch] = edges(0)
    one_out[local_ch] = edges(1).astype(BF16)
    two_out[local_ch] = edges(2).astype(BF16)
    if merged:
        three_out[local_ch] = jnp.where(low_three, edges(-1), edges(3)).astype(BF16)
    else:
        three_out[local_ch] = edges(3).astype(BF16)
    minus_out[0] = edges(-1).astype(BF16)


def hidden_kernel(layer_ref, before_ref, after_ref, weight_ref, slab_ref, hidden_ref, wide_ref):
    images, channels, tile_w, block_rows = layer_ref.shape
    wide_ref[...] = layer_ref[...].astype(F32).reshape(wide_ref.shape)
    last_row = lax.axis_index("row") == lax.axis_size("row") - 1
    local_ch = before_ref.shape[0] - 1
    before = before_ref[local_ch].astype(F32).T
    after = jnp.where(last_row, 0.0, after_ref[local_ch].astype(F32)).T
    for x in range(tile_w):
        for n in range(images):
            rows = wide_ref[pl.ds(n * channels * tile_w + x, channels, stride=tile_w), :]
            part = slice(n * channels, (n + 1) * channels)
            for b in range(3):
                slab_ref[x, b * channels : (b + 1) * channels, n * block_rows : (n + 1) * block_rows] = tap(
                    rows, b, before[part, x : x + 1], after[part, x : x + 1]
                ).astype(BF16)
    weights = first_weights(weight_ref)
    for x in range(1, tile_w - 1):
        hidden_ref[x] = hidden_row(weights, [slab_ref[x + a - 1] for a in range(3)])


def first_weights(weight_ref):
    return [jnp.concatenate([weight_ref[a, b] for b in range(3)], axis=1) for a in range(3)]


def hidden_row(weights, slabs):
    total = None
    for w, s in zip(weights, slabs):
        product = jnp.dot(w, s, preferred_element_type=F32)
        total = product if total is None else total + product
    return jnp.maximum(total, 0.0).astype(BF16)


def combine_kernel(swap, left_ref, own_ref, one_ref, two_ref, three_ref, minus_ref, layer_ref, before_ref, after_ref,
                   grad_ref, edge_ref, *rest):
    sends, (wide_ref, layer_wide, small_ref) = rest[:-3], rest[-3:]
    images, channels, tile_w, block_rows = layer_ref.shape
    local_ch = left_ref.shape[0]
    rows = local_ch * tile_w
    shape = (rows, block_rows)
    left = left_ref[...]
    right = own_ref[...] + one_ref[...].astype(F32) + two_ref[...].astype(F32) + three_ref[...].astype(F32)
    edge = right[local_ch] + minus_ref[0].astype(F32)
    outside = lax.broadcasted_iota(jnp.int32, edge.shape, 1) < jnp.where(lax.axis_index("row") == 0, local_ch, 0)
    edge = jnp.where(outside, 0.0, edge)
    right = right[:local_ch].astype(BF16)
    grad_ref[0] = left
    grad_ref[1] = right
    edge_ref[...] = edge
    wide_ref[:rows] = left.astype(F32).reshape(shape)
    wide_ref[rows:] = right.astype(F32).reshape(shape)
    layer_wide[...] = layer_ref[...].astype(F32).reshape(layer_wide.shape)
    last_row = lax.axis_index("row") == lax.axis_size("row") - 1
    small_ref[0] = before_ref[local_ch].astype(F32)
    small_ref[1] = jnp.where(last_row, 0.0, after_ref[local_ch].astype(F32))
    small_ref[2] = edge
    col = lax.axis_index("col")
    picks = [jnp.where(col == 0, tile_w - 1, 0)] if swap else [tile_w - 1, 0]
    all_in, all_grad = (images * channels, images * local_ch)
    spare = sends[0].shape[0] - all_in - all_grad
    sub = lax.broadcasted_iota(jnp.int32, (spare, block_rows), 0)
    for x, send_ref in zip(picks, sends):
        send_ref[:all_in] = layer_wide[pl.ds(x, all_in, stride=tile_w), :].astype(BF16)
        send_ref[all_in : all_in + all_grad] = wide_ref[pl.ds(x, all_grad, stride=tile_w), :].astype(BF16)
        corners = jnp.zeros((spare, block_rows), F32)
        for j in range(3):
            line = small_ref[j, pl.ds(x, 1), :]
            corners = jnp.where(sub == j, jnp.broadcast_to(line, corners.shape), corners)
        send_ref[all_in + all_grad :] = corners.astype(BF16)


def second_weights(weight_ref, chan, local_ch):
    first = pl.multiple_of(chan * local_ch, local_ch)
    result = []
    for a in range(3):
        parts = []
        for b in range(3):
            w = weight_ref[2 - a, 2 - b, pl.ds(first, local_ch), :].astype(F32)
            half = w.shape[1] // 2
            parts.append(jnp.where(chan == 0, w, jnp.concatenate([w[:, half:], w[:, :half]], axis=1)))
        result.append(jnp.concatenate(parts, axis=0).T.astype(BF16))
    return result


def edge_columns(edge, local_ch, n):
    at = (2, 3) if n == 0 else (0, 1)
    return tuple(edge[k * local_ch : (k + 1) * local_ch] for k in at)


def inner_kernel(grad_ref, edge_ref, hidden_ref, weight_ref, slab_ref, mine_ref, other_ref, second_ref, wide_ref):
    images, local_ch, tile_w, block_rows = grad_ref.shape
    wide_ref[...] = grad_ref[...].astype(F32).reshape(wide_ref.shape)
    edge = edge_ref[...].T
    for x in range(tile_w):
        for n in range(images):
            rows = wide_ref[pl.ds(n * local_ch * tile_w + x, local_ch, stride=tile_w), :]
            before, after = edge_columns(edge, local_ch, n)
            for b in range(3):
                slab_ref[x, b * local_ch : (b + 1) * local_ch, n * block_rows : (n + 1) * block_rows] = tap(
                    rows, b, before[:, x : x + 1], after[:, x : x + 1]
                ).astype(BF16)
    weights = second_weights(weight_ref, lax.axis_index("chan"), local_ch)
    sums = [None] * 3
    for x in range(1, tile_w - 1):
        total = None
        for a in range(3):
            slab = slab_ref[x + a - 1]
            product = jnp.dot(weights[a], slab, preferred_element_type=F32)
            total = product if total is None else total + product
            product = nt(slab, hidden_ref[x])
            sums[a] = product if sums[a] is None else sums[a] + product
        mine_ref[x] = total[:local_ch]
        other_ref[x] = total[local_ch:].astype(BF16)
    for a in range(3):
        second_ref[a] = sums[a]


def outer_kernel(before_ref, after_ref, layer_slab, grad_slab, hidden_ref, w_first_ref, w_second_ref,
                 inner_mine, inner_other, inner_second,
                 layer_edge, hidden_edge, mine_ref, other_ref, second_ref, grad_edge):
    tile_w, triple, lanes = layer_slab.shape
    channels = triple // 3
    local_ch = grad_slab.shape[1] // 3
    images = 2
    block_rows = lanes // images
    all_in, all_grad = (images * channels, images * local_ch)
    col = lax.axis_index("col")
    present = (col > 0, col < lax.axis_size("col") - 1)
    for side, (ref, ok) in enumerate(zip((before_ref, after_ref), present)):
        block = jnp.where(ok, ref[...].astype(F32), 0.0)
        corners = block[all_in + all_grad : all_in + all_grad + 8].T
        edge = corners[:, 2:3]
        for n in range(images):
            lanes_here = slice(n * block_rows, (n + 1) * block_rows)
            part = slice(n * channels, (n + 1) * channels)
            for b in range(3):
                layer_edge[side, b * channels : (b + 1) * channels, lanes_here] = tap(
                    block[part], b, corners[part, 0:1], corners[part, 1:2]
                ).astype(BF16)
            rows = block[all_in + n * local_ch : all_in + (n + 1) * local_ch]
            before, after = edge_columns(edge, local_ch, n)
            for b in range(3):
                grad_edge[side, b * local_ch : (b + 1) * local_ch, lanes_here] = tap(
                    rows, b, before, after
                ).astype(BF16)

    def at(own, halo, p):
        return halo[0] if p < 0 else halo[1] if p >= tile_w else own[p]

    first = first_weights(w_first_ref)
    second = second_weights(w_second_ref, lax.axis_index("chan"), local_ch)
    sums = [inner_second[a] for a in range(3)]
    mine_ref[...] = inner_mine[...]
    other_ref[...] = inner_other[...]
    for side, x in enumerate((0, tile_w - 1)):
        hidden = hidden_row(first, [at(layer_slab, layer_edge, x + a - 1) for a in range(3)])
        hidden_edge[side] = hidden
        total = None
        for a in range(3):
            slab = at(grad_slab, grad_edge, x + a - 1)
            product = jnp.dot(second[a], slab, preferred_element_type=F32)
            total = product if total is None else total + product
            sums[a] = sums[a] + nt(slab, hidden)
        mine_ref[x] = total[:local_ch]
        other_ref[x] = total[local_ch:].astype(BF16)
    for a in range(3):
        second_ref[a] = sums[a]


def first_kernel(mine_ref, arrived_ref, hidden_ref, hidden_edge, layer_slab, layer_edge, second_ref, out_ref):
    tile_w, local_ch, lanes = mine_ref.shape
    channels = layer_slab.shape[1] // 3
    first = pl.multiple_of(lax.axis_index("chan") * local_ch, local_ch)
    sums = [None] * 3
    for x in range(tile_w):
        if x == 0 or x == tile_w - 1:
            hidden = hidden_edge[0 if x == 0 else 1, pl.ds(first, local_ch), :]
        else:
            hidden = hidden_ref[x, pl.ds(first, local_ch), :]
        total = mine_ref[x] + arrived_ref[x].astype(F32)
        grad = jnp.where(hidden.astype(F32) > 0, total, 0.0).astype(BF16)
        for a in range(3):
            p = x + a - 1
            slab = layer_edge[0] if p < 0 else layer_edge[1] if p >= tile_w else layer_slab[p]
            product = nt(grad, slab)
            sums[a] = product if sums[a] is None else sums[a] + product
    for a in range(3):
        for b in range(3):
            one = sums[a][:, b * channels : (b + 1) * channels]
            two = second_ref[2 - a, (2 - b) * local_ch : (3 - b) * local_ch, :]
            out_ref[3 * a + b] = jnp.concatenate([one, two], axis=1).astype(out_ref.dtype)


def swapped(block, axis, step=1):
    return lax.ppermute(block, axis, [(i, i ^ step) for i in range(lax.axis_size(axis))])


def summed_over(partial, axis):
    peers = lax.axis_size(axis)
    step = 1
    while step < peers:
        rounded = lax.reduce_precision(partial, 8, 7)
        partial = rounded + swapped(rounded.astype(BF16), axis, step).astype(F32)
        step *= 2
    return partial


def body(layer_input, features, vol_target, offsets, w_first, w_second):
    images, channels, tile_w, block_rows = layer_input.shape
    local_ch = features.shape[1]
    groups = vol_target.shape[0]
    lanes = images * block_rows
    tile = (tile_w, block_rows)
    plain, framed = ((local_ch + k, *tile) for k in (0, 1))
    merged = lax.axis_size("row") == MAXOFF + 2
    swap = lax.axis_size("col") == 2
    w_first = w_first.transpose(2, 3, 0, 1)
    w_second = w_second.transpose(2, 3, 0, 1)

    up, down = call(pack_kernel, [(framed, BF16)] * 2, layer_input, features, name="pack")
    two = moved(features[1], "row", 2)
    if merged:
        three = below = moved(down, "row", MAXOFF + 1, -1)
    else:
        three = moved(features[1], "row", MAXOFF + 1)
        below = moved(down, "row", -1)
    one = moved(up, "row", 1)

    size = local_ch // groups
    left_grad, own, out_one, out_two, out_three, out_minus = call(
        functools.partial(correlation_kernel, merged),
        [(plain, BF16), (framed, F32)] + [(framed, BF16)] * 3 + [((1, *tile), BF16)],
        offsets, features, one, two, three, vol_target, smem=1, name="correlate", flops=1 << 26,
        scratch=[pltpu.VMEM((DISP, size, *tile), F32), pltpu.VMEM((DISP, *tile), F32)],
    )
    if merged:
        back_three = moved(out_three, "row", -MAXOFF - 1, 1)
        back_minus = jnp.zeros((1, *tile), BF16)
    else:
        back_three = moved(out_three, "row", -MAXOFF - 1)
        back_minus = moved(out_minus, "row", 1)
    back_one = moved(out_one, "row", -1)
    back_two = moved(out_two, "row", -2)

    slab_shape, hidden_shape = ((3 * channels, lanes), (channels, lanes))
    layer_slab, hidden = call(
        hidden_kernel, [((tile_w, *slab_shape), BF16), ((tile_w, *hidden_shape), BF16)],
        layer_input, one, below, w_first, name="hidden", flops=1 << 28,
        scratch=[pltpu.VMEM((images * channels * tile_w, block_rows), F32)],
    )
    message = ((images * (channels + local_ch) + 16, block_rows), BF16)
    grad_features, edge, *sends = call(
        functools.partial(combine_kernel, swap),
        [((images, *plain), BF16), (tile, F32)] + [message] * (1 if swap else 2),
        left_grad, own, back_one, back_two, back_three, back_minus, layer_input, one, below, name="combine",
        scratch=[pltpu.VMEM((images * local_ch * tile_w, block_rows), F32),
                 pltpu.VMEM((images * channels * tile_w, block_rows), F32),
                 pltpu.VMEM((3, *tile), F32)],
    )
    if swap:
        before = after = swapped(sends[0], "col")
    else:
        before, after = (moved(sends[0], "col", 1), moved(sends[1], "col", -1))
    half = (tile_w, local_ch, lanes)
    sums = (3, 3 * local_ch, channels)
    grad_slab, mine, other, second = call(
        inner_kernel, [((tile_w, 3 * local_ch, lanes), BF16), (half, F32), (half, BF16), (sums, F32)],
        grad_features, edge, hidden, w_second, name="inner", flops=1 << 28,
        scratch=[pltpu.VMEM((images * local_ch * tile_w, block_rows), F32)],
    )
    layer_edge, hidden_edge, mine, other, second = call(
        outer_kernel,
        [((2, *slab_shape), BF16), ((2, *hidden_shape), BF16), (half, F32), (half, BF16), (sums, F32)],
        before, after, layer_slab, grad_slab, hidden, w_first, w_second, mine, other, second, name="outer",
        flops=1 << 27, scratch=[pltpu.VMEM((2, 3 * local_ch, lanes), BF16)],
    )
    arrived = swapped(other, "chan")
    partial, = call(
        first_kernel, [((9, local_ch, 2 * channels), F32)],
        mine, arrived, hidden, hidden_edge, layer_slab, layer_edge, second, name="first", flops=1 << 27,
    )
    for axis in ("col", "row"):
        partial = summed_over(partial, axis)
    factor = 1.0 / math.sqrt(
        2.0 * tile_w * lax.axis_size("col") * block_rows * lax.axis_size("row")
    )
    both = lax.all_gather(partial * factor, "chan", axis=1, tiled=True)
    both = both.reshape(3, 3, channels, 2 * channels).transpose(2, 3, 0, 1)
    return (grad_features, both[:, :channels], both[:, channels:])


def solution(mesh):
    return jax.shard_map(
        body,
        mesh=mesh,
        in_specs=(
            P(None, None, ("groups", "col"), "row"),
            P(None, "chan", ("groups", "col"), "row"),
            P("chan", None, ("groups", "col"), "row"),
            P("row", ("groups", "col")),
            P(),
            P(),
        ),
        out_specs=(
            P(None, "chan", ("groups", "col"), "row"),
            P("groups", None, None, None),
            P("groups", None, None, None),
        ),
        check_vma=False,
    )
```

```python
import functools
import math

import jax
import jax.numpy as jnp
from jax import lax
from jax.experimental import pallas as pl
from jax.experimental.pallas import tpu as pltpu
from jax.sharding import PartitionSpec as P


DISP = 40
MAXOFF = 2
F32 = jnp.float32
BF16 = jnp.bfloat16
SPACE = 12 << 20


def call(kernel, outs, *args, smem=0, far=False, scratch=(), flops=1 << 20):
    whole = pl.BlockSpec(memory_space=pltpu.VMEM)
    given = pl.BlockSpec(memory_space=pltpu.HBM) if far else whole
    return pl.pallas_call(
        kernel,
        in_specs=[pl.BlockSpec(memory_space=pltpu.SMEM)] * smem + [given] * (len(args) - smem),
        out_specs=[whole] * len(outs),
        out_shape=[jax.ShapeDtypeStruct(s, t) for s, t in outs],
        scratch_shapes=list(scratch),
        compiler_params=pltpu.CompilerParams(vmem_limit_bytes=SPACE),
        cost_estimate=pl.CostEstimate(flops=flops, bytes_accessed=1 << 20, transcendentals=0),
    )(*args)


def routes():
    peers = lax.axis_size("row")
    if peers == MAXOFF + 2 and peers & (peers - 1) == 0:
        return [("swap", mask) for mask in range(1, peers)]
    return [("line", k) for k in (*range(1, MAXOFF + 2), -1)]


def distance(route):
    kind, value = route
    if kind == "line":
        return value
    row = lax.axis_index("row")
    return row - (row ^ value)


def delivered(block, route, sign):
    kind, value = route
    if kind == "swap":
        return swapped(block, "row", value)
    return moved(block, "row", sign * value)


def moved(block, axis, distance):
    peers = lax.axis_size(axis)
    return lax.ppermute(block, axis, [(i - distance, i) for i in range(peers) if 0 <= i - distance < peers])


def tap(rows, b, before, after):
    if b == 1:
        return rows
    lane = lax.broadcasted_iota(jnp.int32, rows.shape, 1)
    last = rows.shape[1] - 1
    if b == 0:
        return jnp.where(lane == 0, jnp.broadcast_to(before, rows.shape), pltpu.roll(rows, 1, 1))
    return jnp.where(lane == last, jnp.broadcast_to(after, rows.shape), pltpu.roll(rows, last, 1))


def nt(a, b):
    return lax.dot_general(a, b, (((1,), (1,)), ((), ())), preferred_element_type=F32)


def fetch_kernel(*refs):
    count = len(refs) // 2
    sources, targets, sems = refs[:count], refs[count:-1], refs[-1]
    copies = [pltpu.make_async_copy(s, t, sems.at[i]) for i, (s, t) in enumerate(zip(sources, targets))]
    for copy in copies:
        copy.start()
    for copy in copies:
        copy.wait()


def pack_kernel(routing, layer_hbm, features_hbm, *rest):
    out_refs, (layer_ref, features_ref, sems) = rest[:-3], rest[-3:]
    images, channels, tile_w, block_rows = layer_ref.shape
    local_ch = features_ref.shape[0]
    copies = [pltpu.make_async_copy(features_hbm.at[1], features_ref, sems.at[images])]
    for n in range(images):
        copies.append(pltpu.make_async_copy(layer_hbm.at[n], layer_ref.at[n], sems.at[n]))
    for copy in copies:
        copy.start()
    for copy in copies:
        copy.wait()
    shape = (tile_w, block_rows)
    lane = lax.broadcasted_iota(jnp.int32, shape, 1)
    first = jnp.zeros(shape, F32)
    last = jnp.zeros(shape, F32)
    for n in range(images):
        for c in range(channels):
            tile = layer_ref[n, c].astype(F32)
            here = lane == n * channels + c
            first = jnp.where(here, jnp.broadcast_to(tile[:, :1], shape), first)
            last = jnp.where(here, jnp.broadcast_to(tile[:, block_rows - 1 :], shape), last)
    for route, out_ref in zip(routing, out_refs):
        ahead = distance(route) if route[0] == "line" else -distance(route)
        out_ref[:local_ch] = features_ref[...]
        out_ref[local_ch] = jnp.where(ahead == 1, last, jnp.where(ahead == -1, first, 0.0)).astype(BF16)


def correlation_kernel(routing, offset_ref, features_ref, target_ref, *rest):
    count = len(routing)
    block_refs, (left_out, own_out) = rest[:count], rest[count : count + 2]
    out_refs, (moved_ref, residual_ref) = rest[count + 2 : -2], rest[-2:]
    ahead = [distance(route) for route in routing]
    offset = offset_ref[0, 0]
    local_ch, tile_w, block_rows = features_ref.shape[1:]
    groups = target_ref.shape[0]
    size = local_ch // groups
    inv_size = 1.0 / size
    shape = (tile_w, block_rows)
    lane = lax.broadcasted_iota(jnp.int32, shape, 1)
    zero = jnp.zeros(shape, F32)

    def column(tile, at, kind, c, into):
        picked = jnp.broadcast_to(tile[:, at : at + 1], shape)
        return jnp.where(lane == kind * local_ch + c, picked, into)

    def one_group(g, edges):
        end_main, end_spill, start_main, end_left, start_left = edges
        base = g * size

        def scaled_left(c):
            return features_ref[0, base + c].astype(F32) * inv_size

        left, main, spill = [], [], []
        for c in range(size):
            here = features_ref[1, base + c].astype(F32)
            before = zero
            for k, block_ref in zip(ahead, block_refs):
                block = block_ref[base + c].astype(F32)
                here = jnp.where(k == offset, block, here)
                before = jnp.where(k == offset + 1, block, before)
            left.append(scaled_left(c))
            main.append(here)
            spill.append(before)
        for d in range(DISP):
            products = []
            for c in range(size):
                moved = main[c]
                if d:
                    moved = pltpu.roll(jnp.where(lane >= block_rows - d, spill[c], moved), d, 1)
                moved_ref[d, c] = moved
                products.append(left[c] * moved)
            while len(products) > 1:
                products = [sum(products[i : i + 2]) for i in range(0, len(products), 2)]
            residual_ref[d] = products[0] - target_ref[g, d].astype(F32)
        for first in range(0, size, 2):
            channels = range(first, min(first + 2, size))
            left_grad = {c: zero for c in channels}
            whole_grad = {c: zero for c in channels}
            spill_grad = {c: zero for c in channels}
            scaled = {c: scaled_left(c) for c in channels}
            for d in range(DISP):
                residual = residual_ref[d]
                for c in channels:
                    left_grad[c] = left_grad[c] + residual * moved_ref[d, c]
                    part = residual * scaled[c]
                    if d:
                        part = pltpu.roll(part, block_rows - d, 1)
                        spill_grad[c] = spill_grad[c] + jnp.where(lane >= block_rows - d, part, 0.0)
                    whole_grad[c] = whole_grad[c] + part
            for c in channels:
                ch = base + c
                main_grad = whole_grad[c] - spill_grad[c]
                final = (left_grad[c] * inv_size).astype(BF16)
                left_out[ch] = final
                final = final.astype(F32)
                own_out[ch] = jnp.where(offset == 0, main_grad, 0.0)
                for k, out_ref in zip(ahead, out_refs):
                    out_ref[ch] = jnp.where(
                        offset + 1 == k, spill_grad[c], jnp.where(offset == k, main_grad, 0.0)
                    ).astype(BF16)
                end_main = column(main_grad, block_rows - 1, 0, ch, end_main)
                end_spill = column(spill_grad[c], block_rows - 1, 0, ch, end_spill)
                start_main = column(main_grad, 0, 1, ch, start_main)
                end_left = column(final, block_rows - 1, 2, ch, end_left)
                start_left = column(final, 0, 3, ch, start_left)
        return end_main, end_spill, start_main, end_left, start_left

    end_main, end_spill, start_main, end_left, start_left = lax.fori_loop(
        0, groups, one_group, (zero,) * 5
    )

    def edges(k):
        tile = jnp.where(offset == k + 1, end_main, 0.0) + jnp.where(offset == k, end_spill, 0.0)
        tile = tile + jnp.where(offset == k - 1, start_main, 0.0)
        return tile + jnp.where(k == -1, end_left, jnp.where(k == 1, start_left, 0.0))

    own_out[local_ch] = edges(0)
    for k, out_ref in zip(ahead, out_refs):
        out_ref[local_ch] = edges(k).astype(BF16)


def hidden_kernel(routing, layer_ref, first_ref, second_ref, *rest):
    block_refs, (slab_ref, hidden_ref, first_out, second_out) = rest[: len(routing)], rest[len(routing) :][:4]
    rest = rest[len(routing) + 4 :]
    rows_refs, corner_refs, (wide_ref, small_ref) = rest[: len(rest) // 2 - 1], rest[len(rest) // 2 - 1 : -2], rest[-2:]
    images, channels, tile_w, block_rows = layer_ref.shape
    wide_ref[...] = layer_ref[...].astype(F32).reshape(wide_ref.shape)
    before = after = jnp.zeros((tile_w, block_rows), F32)
    for route, block_ref in zip(routing, block_refs):
        k = distance(route)
        tile = block_ref[block_ref.shape[0] - 1].astype(F32)
        before = jnp.where(k == 1, tile, before)
        after = jnp.where(k == -1, tile, after)
    small_ref[0] = before
    small_ref[1] = after
    before, after = before.T, after.T
    for x in range(tile_w):
        for n in range(images):
            rows = wide_ref[pl.ds(n * channels * tile_w + x, channels, stride=tile_w), :]
            part = slice(n * channels, (n + 1) * channels)
            for b in range(3):
                slab_ref[x, b * channels : (b + 1) * channels, n * block_rows : (n + 1) * block_rows] = tap(
                    rows, b, before[part, x : x + 1], after[part, x : x + 1]
                ).astype(BF16)
    weights = first_weights(first_ref)
    local_ch = channels // lax.axis_size("chan")
    for a, (w, v) in enumerate(zip(weights, second_weights(second_ref, lax.axis_index("chan"), local_ch))):
        first_out[a] = w
        second_out[a] = v
    for x in range(1, tile_w - 1):
        hidden_ref[x] = hidden_row(weights, [slab_ref[x + a - 1] for a in range(3)])
    for x, rows_ref, corner_ref in zip(border_rows(len(rows_refs), tile_w), rows_refs, corner_refs):
        rows_ref[...] = wide_ref[pl.ds(x, images * channels, stride=tile_w), :].astype(BF16)
        corner_ref[...] = stacked_lines([small_ref[j, pl.ds(x, 1), :] for j in range(2)], tile_w)


def border_rows(messages, tile_w):
    if messages == 1:
        return [jnp.where(lax.axis_index("col") == 0, tile_w - 1, 0)]
    return [tile_w - 1, 0]


def stacked_lines(lines, height):
    shape = (height, lines[0].shape[1])
    sub = lax.broadcasted_iota(jnp.int32, shape, 0)
    tile = jnp.zeros(shape, F32)
    for j, line in enumerate(lines):
        tile = jnp.where(sub == j, jnp.broadcast_to(line, shape), tile)
    return tile


def first_weights(weight_ref):
    return [jnp.concatenate([weight_ref[a, b] for b in range(3)], axis=1) for a in range(3)]


def hidden_row(weights, slabs):
    total = None
    for w, s in zip(weights, slabs):
        product = jnp.dot(w, s, preferred_element_type=F32)
        total = product if total is None else total + product
    return jnp.maximum(total, 0.0).astype(BF16)


def combine_kernel(arrivals, left_ref, own_ref, *rest):
    block_refs, rest = rest[:arrivals], rest[arrivals:]
    count = (len(rest) - 3) // 3
    rows_refs, corner_refs = rest[:count], rest[count : 2 * count]
    wide_ref, edge_ref = rest[2 * count : 2 * count + 2]
    sends, small_ref = rest[2 * count + 2 : -1], rest[-1]
    local_ch, tile_w, block_rows = left_ref.shape
    images = wide_ref.shape[0] // (local_ch * tile_w)
    rows = local_ch * tile_w
    shape = (rows, block_rows)
    lane = lax.broadcasted_iota(jnp.int32, (tile_w, block_rows), 1)
    left = left_ref[...]
    total = own_ref[...]
    for block_ref in block_refs:
        total = total + block_ref[...].astype(F32)
    right, edge = total[:local_ch].astype(BF16), total[local_ch]
    wide_ref[:rows] = left.astype(F32).reshape(shape)
    wide_ref[rows:] = right.astype(F32).reshape(shape)
    outside = lane < jnp.where(lax.axis_index("row") == 0, local_ch, 0)
    edge = jnp.where(outside, 0.0, edge)
    edge_ref[...] = edge
    small_ref[...] = edge
    all_in, all_grad = (rows_refs[0].shape[0], images * local_ch)
    for x, rows_ref, corner_ref, send_ref in zip(border_rows(count, tile_w), rows_refs, corner_refs, sends):
        send_ref[:all_in] = rows_ref[...]
        send_ref[all_in : all_in + all_grad] = wide_ref[pl.ds(x, all_grad, stride=tile_w), :].astype(BF16)
        lines = [corner_ref[0:1, :], corner_ref[1:2, :], small_ref[pl.ds(x, 1), :]]
        send_ref[all_in + all_grad :] = stacked_lines(lines, send_ref.shape[0] - all_in - all_grad).astype(BF16)


def second_weights(weight_ref, chan, local_ch):
    first = pl.multiple_of(chan * local_ch, local_ch)
    result = []
    for a in range(3):
        parts = []
        for b in range(3):
            w = weight_ref[2 - a, 2 - b, pl.ds(first, local_ch), :].astype(F32)
            half = w.shape[1] // 2
            parts.append(jnp.where(chan == 0, w, jnp.concatenate([w[:, half:], w[:, :half]], axis=1)))
        result.append(jnp.concatenate(parts, axis=0).T.astype(BF16))
    return result


def edge_columns(edge, local_ch, n):
    at = (2, 3) if n == 0 else (0, 1)
    return tuple(edge[k * local_ch : (k + 1) * local_ch] for k in at)


def inner_kernel(wide_ref, edge_ref, hidden_ref, weight_ref, slab_ref, mine_ref, other_ref, second_ref, grad_ref):
    images, local_ch, tile_w, block_rows = grad_ref.shape
    grad_ref[...] = wide_ref[...].reshape(grad_ref.shape).astype(BF16)
    edge = edge_ref[...].T
    for x in range(tile_w):
        for n in range(images):
            rows = wide_ref[pl.ds(n * local_ch * tile_w + x, local_ch, stride=tile_w), :]
            before, after = edge_columns(edge, local_ch, n)
            for b in range(3):
                slab_ref[x, b * local_ch : (b + 1) * local_ch, n * block_rows : (n + 1) * block_rows] = tap(
                    rows, b, before[:, x : x + 1], after[:, x : x + 1]
                ).astype(BF16)
    weights = [weight_ref[a] for a in range(3)]
    sums = [None] * 3
    for x in range(1, tile_w - 1):
        total = None
        for a in range(3):
            slab = slab_ref[x + a - 1]
            total = added(total, jnp.dot(weights[a], slab, preferred_element_type=F32))
            sums[a] = added(sums[a], nt(slab, hidden_ref[x]))
        mine_ref[x - 1] = total[:local_ch]
        other_ref[x - 1] = total[local_ch:].astype(BF16)
    for a in range(3):
        second_ref[a] = sums[a]


def added(total, product):
    return product if total is None else total + product


def inner_first_kernel(mine_ref, arrived_ref, hidden_ref, layer_slab, out_ref):
    rows, local_ch, _ = mine_ref.shape
    first = pl.multiple_of(lax.axis_index("chan") * local_ch, local_ch)
    sums = [None] * 3
    for x in range(1, rows + 1):
        grad = masked(mine_ref[x - 1], arrived_ref[x - 1], hidden_ref[x, pl.ds(first, local_ch), :])
        for a in range(3):
            sums[a] = added(sums[a], nt(grad, layer_slab[x + a - 1]))
    for a in range(3):
        out_ref[a] = sums[a]


def masked(mine, arrived, hidden):
    return jnp.where(hidden.astype(F32) > 0, mine + arrived.astype(F32), 0.0).astype(BF16)


def halo_at(own, halo, p):
    return halo[0] if p < 0 else halo[1] if p >= own.shape[0] else own[p]


def outer_kernel(before_ref, after_ref, layer_slab, grad_slab, w_first_ref, w_second_ref,
                 layer_edge, grad_edge, hidden_edge, mine_ref, other_ref):
    tile_w, triple, lanes = layer_slab.shape
    channels = triple // 3
    local_ch = grad_slab.shape[1] // 3
    images = 2
    block_rows = lanes // images
    all_in, all_grad = (images * channels, images * local_ch)
    col = lax.axis_index("col")
    present = (col > 0, col < lax.axis_size("col") - 1)
    for side, (ref, ok) in enumerate(zip((before_ref, after_ref), present)):
        block = jnp.where(ok, ref[...].astype(F32), 0.0)
        corners = block[all_in + all_grad : all_in + all_grad + 8].T
        edge = corners[:, 2:3]
        for n in range(images):
            lanes_here = slice(n * block_rows, (n + 1) * block_rows)
            part = slice(n * channels, (n + 1) * channels)
            rows = block[all_in + n * local_ch : all_in + (n + 1) * local_ch]
            before, after = edge_columns(edge, local_ch, n)
            for b in range(3):
                layer_edge[side, b * channels : (b + 1) * channels, lanes_here] = tap(
                    block[part], b, corners[part, 0:1], corners[part, 1:2]
                ).astype(BF16)
                grad_edge[side, b * local_ch : (b + 1) * local_ch, lanes_here] = tap(
                    rows, b, before, after
                ).astype(BF16)
    first = [w_first_ref[a] for a in range(3)]
    second = [w_second_ref[a] for a in range(3)]
    for side, x in enumerate((0, tile_w - 1)):
        hidden_edge[side] = hidden_row(first, [halo_at(layer_slab, layer_edge, x + a - 1) for a in range(3)])
        total = None
        for a in range(3):
            slab = halo_at(grad_slab, grad_edge, x + a - 1)
            total = added(total, jnp.dot(second[a], slab, preferred_element_type=F32))
        mine_ref[side] = total[:local_ch]
        other_ref[side] = total[local_ch:].astype(BF16)


def second_kernel(inner_ref, grad_slab, grad_edge, hidden_edge, out_ref):
    tile_w = grad_slab.shape[0]
    for a in range(3):
        total = inner_ref[a]
        for side, x in enumerate((0, tile_w - 1)):
            total = total + nt(halo_at(grad_slab, grad_edge, x + a - 1), hidden_edge[side])
        out_ref[a] = total


def last_kernel(mine_ref, arrived_ref, hidden_edge, layer_slab, layer_edge, inner_ref, second_ref, out_ref):
    tile_w = layer_slab.shape[0]
    local_ch = mine_ref.shape[1]
    channels = layer_slab.shape[1] // 3
    first = pl.multiple_of(lax.axis_index("chan") * local_ch, local_ch)
    sums = [inner_ref[a] for a in range(3)]
    for side, x in enumerate((0, tile_w - 1)):
        grad = masked(mine_ref[side], arrived_ref[side], hidden_edge[side, pl.ds(first, local_ch), :])
        for a in range(3):
            sums[a] = sums[a] + nt(grad, halo_at(layer_slab, layer_edge, x + a - 1))
    for a in range(3):
        for b in range(3):
            one = sums[a][:, b * channels : (b + 1) * channels]
            two = second_ref[2 - a, (2 - b) * local_ch : (3 - b) * local_ch, :]
            out_ref[3 * a + b] = jnp.concatenate([one, two], axis=1)


def finish_kernel(factor, own_ref, arrived_ref, first_ref, second_ref):
    local_ch = own_ref.shape[1]
    channels = first_ref.shape[3]
    chan = lax.axis_index("chan")
    for ref, at in ((own_ref, chan), (arrived_ref, 1 - chan)):
        here = pl.ds(pl.multiple_of(at * local_ch, local_ch), local_ch)
        for a in range(3):
            for b in range(3):
                block = ref[3 * a + b] * factor
                first_ref[a, b, here, :] = block[:, :channels]
                second_ref[a, b, here, :] = block[:, channels:]


def swapped(block, axis, step=1):
    return lax.ppermute(block, axis, [(i, i ^ step) for i in range(lax.axis_size(axis))])


def exchanged(partial, axis, *steps):
    rounded = lax.reduce_precision(partial, 8, 7)
    sent = rounded.astype(BF16)
    terms = [rounded] + [swapped(sent, axis, step).astype(F32) for step in steps]
    while len(terms) > 1:
        terms = [sum(terms[i : i + 2]) for i in range(0, len(terms), 2)]
    return terms[0]


def summed(partial):
    peers = lax.axis_size("row")
    step = 1
    while step < peers:
        if step * 2 < peers:
            partial = exchanged(partial, "row", step, 2 * step, 3 * step)
            step *= 4
        else:
            partial = exchanged(partial, "row", step)
            step *= 2
    peers = lax.axis_size("col")
    step = 1
    while step < peers:
        partial = exchanged(partial, "col", step)
        step *= 2
    return partial


def whole(layer_input, features, vol_target, offsets, w_first, w_second):
    images, channels, tile_w, block_rows = layer_input.shape
    local_ch = features.shape[1]
    groups = vol_target.shape[0]
    lanes = images * block_rows
    tile = (tile_w, block_rows)
    plain, framed = ((local_ch + k, *tile) for k in (0, 1))
    swap = lax.axis_size("col") == 2
    routing = routes()
    w_first = w_first.transpose(2, 3, 0, 1)
    w_second = w_second.transpose(2, 3, 0, 1)

    packed = call(
        functools.partial(pack_kernel, routing), [(framed, BF16)] * len(routing), layer_input, features, far=True,
        scratch=[pltpu.VMEM(layer_input.shape, BF16), pltpu.VMEM(plain, BF16),
                 pltpu.SemaphoreType.DMA((images + 1,))],
    )
    blocks = []
    for block, route in zip(packed, routing):
        blocks.append(delivered(block, route, 1))

    arrays = (vol_target, features, layer_input, w_first, w_second)
    vol_target, features, layer_input, w_first, w_second = call(
        fetch_kernel, [(array.shape, array.dtype) for array in arrays], *arrays, far=True,
        scratch=[pltpu.SemaphoreType.DMA((len(arrays),))],
    )

    size = local_ch // groups
    left_grad, own, *outgoing = call(
        functools.partial(correlation_kernel, routing),
        [(plain, BF16), (framed, F32)] + [(framed, BF16)] * len(routing),
        offsets, features, vol_target, *blocks, smem=1, flops=1 << 26,
        scratch=[pltpu.VMEM((DISP, size, *tile), F32), pltpu.VMEM((DISP, *tile), F32)],
    )
    arrivals = []
    for block, route in zip(outgoing, routing):
        arrivals.append(delivered(block, route, -1))

    messages = 1 if swap else 2
    slab_shape, hidden_shape = ((3 * channels, lanes), (channels, lanes))
    lines = (images * channels, block_rows)
    layer_slab, hidden, w_first, w_second, *border = call(
        functools.partial(hidden_kernel, routing),
        [((tile_w, *slab_shape), BF16), ((tile_w, *hidden_shape), BF16),
         ((3, channels, 3 * channels), BF16), ((3, channels, 3 * local_ch), BF16)]
        + [(lines, BF16)] * messages + [(tile, F32)] * messages,
        layer_input, w_first, w_second, *blocks, flops=1 << 28,
        scratch=[pltpu.VMEM((images * channels * tile_w, block_rows), F32), pltpu.VMEM((2, *tile), F32)],
    )
    message = ((images * (channels + local_ch) + 16, block_rows), BF16)
    wide, edge, *sends = call(
        functools.partial(combine_kernel, len(routing)),
        [((images * local_ch * tile_w, block_rows), F32), (tile, F32)] + [message] * messages,
        left_grad, own, *arrivals, *border,
        scratch=[pltpu.VMEM(tile, F32)],
    )
    if swap:
        before = after = swapped(sends[0], "col")
    else:
        before, after = (moved(sends[0], "col", 1), moved(sends[1], "col", -1))
    middle, rim = (tile_w - 2, local_ch, lanes), (2, local_ch, lanes)
    sums = (3, 3 * local_ch, channels)
    grad_slab, mine, other, second, grad_features = call(
        inner_kernel,
        [((tile_w, 3 * local_ch, lanes), BF16), (middle, F32), (middle, BF16), (sums, F32),
         ((images, *plain), BF16)],
        wide, edge, hidden, w_second, flops=1 << 28,
    )
    arrived = swapped(other, "chan")
    inner_first, = call(
        inner_first_kernel, [((3, local_ch, 3 * channels), F32)],
        mine, arrived, hidden, layer_slab, flops=1 << 28,
    )
    layer_edge, grad_edge, hidden_edge, mine, other = call(
        outer_kernel,
        [((2, *slab_shape), BF16), ((2, 3 * local_ch, lanes), BF16), ((2, *hidden_shape), BF16),
         (rim, F32), (rim, BF16)],
        before, after, layer_slab, grad_slab, w_first, w_second, flops=1 << 27,
    )
    arrived = swapped(other, "chan")
    second, = call(second_kernel, [(sums, F32)], second, grad_slab, grad_edge, hidden_edge, flops=1 << 27)
    partial, = call(
        last_kernel, [((9, local_ch, 2 * channels), F32)],
        mine, arrived, hidden_edge, layer_slab, layer_edge, inner_first, second, flops=1 << 27,
    )
    total = summed(partial)
    factor = 1.0 / math.sqrt(
        2.0 * tile_w * lax.axis_size("col") * block_rows * lax.axis_size("row")
    )
    first, second = call(
        functools.partial(finish_kernel, factor), [((3, 3, channels, channels), F32)] * 2,
        total, swapped(total, "chan"),
    )
    return (grad_features, first.transpose(2, 3, 0, 1), second.transpose(2, 3, 0, 1))


def solution(mesh):
    return jax.shard_map(
        whole,
        mesh=mesh,
        in_specs=(
            P(None, None, ("groups", "col"), "row"),
            P(None, "chan", ("groups", "col"), "row"),
            P("chan", None, ("groups", "col"), "row"),
            P("row", ("groups", "col")),
            P(),
            P(),
        ),
        out_specs=(
            P(None, "chan", ("groups", "col"), "row"),
            P("groups", None, None, None),
            P("groups", None, None, None),
        ),
        check_vma=False,
    )
```

```python
import functools
import math

import jax
import jax.numpy as jnp
from jax import lax
from jax.experimental import pallas as pl
from jax.experimental.pallas import tpu as pltpu
from jax.sharding import PartitionSpec as P


DISP = 40
MAXOFF = 2
F32 = jnp.float32
BF16 = jnp.bfloat16
SPACE = 12 << 20


def call(kernel, outs, *args, smem=0, far=False, scratch=(), flops=1 << 20):
    whole = pl.BlockSpec(memory_space=pltpu.VMEM)
    given = pl.BlockSpec(memory_space=pltpu.HBM) if far else whole
    return pl.pallas_call(
        kernel,
        in_specs=[pl.BlockSpec(memory_space=pltpu.SMEM)] * smem + [given] * (len(args) - smem),
        out_specs=[whole] * len(outs),
        out_shape=[jax.ShapeDtypeStruct(s, t) for s, t in outs],
        scratch_shapes=list(scratch),
        compiler_params=pltpu.CompilerParams(vmem_limit_bytes=SPACE),
        cost_estimate=pl.CostEstimate(flops=flops, bytes_accessed=1 << 20, transcendentals=0),
    )(*args)


def routes():
    peers = lax.axis_size("row")
    if peers == MAXOFF + 2 and peers & (peers - 1) == 0:
        return [("swap", mask) for mask in range(1, peers)]
    return [("line", k) for k in (*range(1, MAXOFF + 2), -1)]


def distance(route):
    kind, value = route
    if kind == "line":
        return value
    row = lax.axis_index("row")
    return row - (row ^ value)


def delivered(block, route, sign):
    kind, value = route
    if kind == "swap":
        return swapped(block, "row", value)
    return moved(block, "row", sign * value)


def moved(block, axis, distance):
    peers = lax.axis_size(axis)
    return lax.ppermute(block, axis, [(i - distance, i) for i in range(peers) if 0 <= i - distance < peers])


def tap(rows, b, before, after):
    if b == 1:
        return rows
    lane = lax.broadcasted_iota(jnp.int32, rows.shape, 1)
    last = rows.shape[1] - 1
    if b == 0:
        return jnp.where(lane == 0, jnp.broadcast_to(before, rows.shape), pltpu.roll(rows, 1, 1))
    return jnp.where(lane == last, jnp.broadcast_to(after, rows.shape), pltpu.roll(rows, last, 1))


def nt(a, b):
    return lax.dot_general(a, b, (((1,), (1,)), ((), ())), preferred_element_type=F32)


def fetch_kernel(*refs):
    count = len(refs) // 2
    sources, targets, sems = refs[:count], refs[count:-1], refs[-1]
    copies = [pltpu.make_async_copy(s, t, sems.at[i]) for i, (s, t) in enumerate(zip(sources, targets))]
    for copy in copies:
        copy.start()
    for copy in copies:
        copy.wait()


def pack_kernel(routing, layer_ref, features_ref, *out_refs):
    images, channels, tile_w, block_rows = layer_ref.shape
    local_ch = features_ref.shape[1]
    shape = (tile_w, block_rows)
    lane = lax.broadcasted_iota(jnp.int32, shape, 1)
    first = jnp.zeros(shape, F32)
    last = jnp.zeros(shape, F32)
    for n in range(images):
        for c in range(channels):
            tile = layer_ref[n, c].astype(F32)
            here = lane == n * channels + c
            first = jnp.where(here, jnp.broadcast_to(tile[:, :1], shape), first)
            last = jnp.where(here, jnp.broadcast_to(tile[:, block_rows - 1 :], shape), last)
    for route, out_ref in zip(routing, out_refs):
        ahead = distance(route) if route[0] == "line" else -distance(route)
        out_ref[:local_ch] = features_ref[1]
        out_ref[local_ch] = jnp.where(ahead == 1, last, jnp.where(ahead == -1, first, 0.0)).astype(BF16)


def correlation_kernel(routing, offset_ref, features_ref, target_ref, *rest):
    count = len(routing)
    block_refs, (left_out, own_out) = rest[:count], rest[count : count + 2]
    out_refs, (moved_ref, residual_ref) = rest[count + 2 : -2], rest[-2:]
    ahead = [distance(route) for route in routing]
    offset = offset_ref[0, 0]
    local_ch, tile_w, block_rows = features_ref.shape[1:]
    groups = target_ref.shape[0]
    size = local_ch // groups
    inv_size = 1.0 / size
    shape = (tile_w, block_rows)
    lane = lax.broadcasted_iota(jnp.int32, shape, 1)
    zero = jnp.zeros(shape, F32)

    def column(tile, at, kind, c, into):
        picked = jnp.broadcast_to(tile[:, at : at + 1], shape)
        return jnp.where(lane == kind * local_ch + c, picked, into)

    def one_group(g, edges):
        end_main, end_spill, start_main, end_left, start_left = edges
        base = g * size

        def scaled_left(c):
            return features_ref[0, base + c].astype(F32) * inv_size

        left, main, spill = [], [], []
        for c in range(size):
            here = features_ref[1, base + c].astype(F32)
            before = zero
            for k, block_ref in zip(ahead, block_refs):
                block = block_ref[base + c].astype(F32)
                here = jnp.where(k == offset, block, here)
                before = jnp.where(k == offset + 1, block, before)
            left.append(scaled_left(c))
            main.append(here)
            spill.append(before)
        for d in range(DISP):
            products = []
            for c in range(size):
                moved = main[c]
                if d:
                    moved = pltpu.roll(jnp.where(lane >= block_rows - d, spill[c], moved), d, 1)
                moved_ref[d, c] = moved
                products.append(left[c] * moved)
            while len(products) > 1:
                products = [sum(products[i : i + 2]) for i in range(0, len(products), 2)]
            residual_ref[d] = products[0] - target_ref[g, d].astype(F32)
        for first in range(0, size, 2):
            channels = range(first, min(first + 2, size))
            left_grad = {c: zero for c in channels}
            whole_grad = {c: zero for c in channels}
            spill_grad = {c: zero for c in channels}
            scaled = {c: scaled_left(c) for c in channels}
            for d in range(DISP):
                residual = residual_ref[d]
                for c in channels:
                    left_grad[c] = left_grad[c] + residual * moved_ref[d, c]
                    part = residual * scaled[c]
                    if d:
                        part = pltpu.roll(part, block_rows - d, 1)
                        spill_grad[c] = spill_grad[c] + jnp.where(lane >= block_rows - d, part, 0.0)
                    whole_grad[c] = whole_grad[c] + part
            for c in channels:
                ch = base + c
                main_grad = whole_grad[c] - spill_grad[c]
                final = (left_grad[c] * inv_size).astype(BF16)
                left_out[ch] = final
                final = final.astype(F32)
                own_out[ch] = jnp.where(offset == 0, main_grad, 0.0)
                for k, out_ref in zip(ahead, out_refs):
                    out_ref[ch] = jnp.where(
                        offset + 1 == k, spill_grad[c], jnp.where(offset == k, main_grad, 0.0)
                    ).astype(BF16)
                end_main = column(main_grad, block_rows - 1, 0, ch, end_main)
                end_spill = column(spill_grad[c], block_rows - 1, 0, ch, end_spill)
                start_main = column(main_grad, 0, 1, ch, start_main)
                end_left = column(final, block_rows - 1, 2, ch, end_left)
                start_left = column(final, 0, 3, ch, start_left)
        return end_main, end_spill, start_main, end_left, start_left

    end_main, end_spill, start_main, end_left, start_left = lax.fori_loop(
        0, groups, one_group, (zero,) * 5
    )

    def edges(k):
        tile = jnp.where(offset == k + 1, end_main, 0.0) + jnp.where(offset == k, end_spill, 0.0)
        tile = tile + jnp.where(offset == k - 1, start_main, 0.0)
        return tile + jnp.where(k == -1, end_left, jnp.where(k == 1, start_left, 0.0))

    own_out[local_ch] = edges(0)
    for k, out_ref in zip(ahead, out_refs):
        out_ref[local_ch] = edges(k).astype(BF16)


def hidden_kernel(routing, layer_ref, first_ref, second_ref, *rest):
    block_refs, (slab_ref, hidden_ref, first_out, second_out) = rest[: len(routing)], rest[len(routing) :][:4]
    rest = rest[len(routing) + 4 :]
    rows_refs, corner_refs, (wide_ref, small_ref) = rest[: len(rest) // 2 - 1], rest[len(rest) // 2 - 1 : -2], rest[-2:]
    images, channels, tile_w, block_rows = layer_ref.shape
    wide_ref[...] = layer_ref[...].astype(F32).reshape(wide_ref.shape)
    before = after = jnp.zeros((tile_w, block_rows), F32)
    for route, block_ref in zip(routing, block_refs):
        k = distance(route)
        tile = block_ref[block_ref.shape[0] - 1].astype(F32)
        before = jnp.where(k == 1, tile, before)
        after = jnp.where(k == -1, tile, after)
    small_ref[0] = before
    small_ref[1] = after
    before, after = before.T, after.T
    for x in range(tile_w):
        for n in range(images):
            rows = wide_ref[pl.ds(n * channels * tile_w + x, channels, stride=tile_w), :]
            part = slice(n * channels, (n + 1) * channels)
            for b in range(3):
                slab_ref[x, b * channels : (b + 1) * channels, n * block_rows : (n + 1) * block_rows] = tap(
                    rows, b, before[part, x : x + 1], after[part, x : x + 1]
                ).astype(BF16)
    weights = first_weights(first_ref)
    local_ch = channels // lax.axis_size("chan")
    for a, (w, v) in enumerate(zip(weights, second_weights(second_ref, lax.axis_index("chan"), local_ch))):
        first_out[a] = w
        second_out[a] = v
    for x in range(1, tile_w - 1):
        hidden_ref[x] = hidden_row(weights, [slab_ref[x + a - 1] for a in range(3)])
    for x, rows_ref, corner_ref in zip(border_rows(len(rows_refs), tile_w), rows_refs, corner_refs):
        rows_ref[...] = wide_ref[pl.ds(x, images * channels, stride=tile_w), :].astype(BF16)
        corner_ref[...] = stacked_lines([small_ref[j, pl.ds(x, 1), :] for j in range(2)], tile_w)


def border_rows(messages, tile_w):
    if messages == 1:
        return [jnp.where(lax.axis_index("col") == 0, tile_w - 1, 0)]
    return [tile_w - 1, 0]


def stacked_lines(lines, height):
    shape = (height, lines[0].shape[1])
    sub = lax.broadcasted_iota(jnp.int32, shape, 0)
    tile = jnp.zeros(shape, F32)
    for j, line in enumerate(lines):
        tile = jnp.where(sub == j, jnp.broadcast_to(line, shape), tile)
    return tile


def first_weights(weight_ref):
    return [jnp.concatenate([weight_ref[a, b] for b in range(3)], axis=1) for a in range(3)]


def hidden_row(weights, slabs):
    total = None
    for w, s in zip(weights, slabs):
        product = jnp.dot(w, s, preferred_element_type=F32)
        total = product if total is None else total + product
    return jnp.maximum(total, 0.0).astype(BF16)


def combine_kernel(arrivals, left_ref, own_ref, *rest):
    block_refs, rest = rest[:arrivals], rest[arrivals:]
    count = (len(rest) - 3) // 3
    rows_refs, corner_refs = rest[:count], rest[count : 2 * count]
    wide_ref, edge_ref = rest[2 * count : 2 * count + 2]
    sends, small_ref = rest[2 * count + 2 : -1], rest[-1]
    local_ch, tile_w, block_rows = left_ref.shape
    images = wide_ref.shape[0] // (local_ch * tile_w)
    rows = local_ch * tile_w
    shape = (rows, block_rows)
    lane = lax.broadcasted_iota(jnp.int32, (tile_w, block_rows), 1)
    left = left_ref[...]
    total = own_ref[...]
    for block_ref in block_refs:
        total = total + block_ref[...].astype(F32)
    right, edge = total[:local_ch].astype(BF16), total[local_ch]
    wide_ref[:rows] = left.astype(F32).reshape(shape)
    wide_ref[rows:] = right.astype(F32).reshape(shape)
    outside = lane < jnp.where(lax.axis_index("row") == 0, local_ch, 0)
    edge = jnp.where(outside, 0.0, edge)
    edge_ref[...] = edge
    small_ref[...] = edge
    all_in, all_grad = (rows_refs[0].shape[0], images * local_ch)
    for x, rows_ref, corner_ref, send_ref in zip(border_rows(count, tile_w), rows_refs, corner_refs, sends):
        send_ref[:all_in] = rows_ref[...]
        send_ref[all_in : all_in + all_grad] = wide_ref[pl.ds(x, all_grad, stride=tile_w), :].astype(BF16)
        lines = [corner_ref[0:1, :], corner_ref[1:2, :], small_ref[pl.ds(x, 1), :]]
        send_ref[all_in + all_grad :] = stacked_lines(lines, send_ref.shape[0] - all_in - all_grad).astype(BF16)


def second_weights(weight_ref, chan, local_ch):
    first = pl.multiple_of(chan * local_ch, local_ch)
    result = []
    for a in range(3):
        parts = []
        for b in range(3):
            w = weight_ref[2 - a, 2 - b, pl.ds(first, local_ch), :].astype(F32)
            half = w.shape[1] // 2
            parts.append(jnp.where(chan == 0, w, jnp.concatenate([w[:, half:], w[:, :half]], axis=1)))
        result.append(jnp.concatenate(parts, axis=0).T.astype(BF16))
    return result


def edge_columns(edge, local_ch, n):
    at = (2, 3) if n == 0 else (0, 1)
    return tuple(edge[k * local_ch : (k + 1) * local_ch] for k in at)


def inner_kernel(wide_ref, edge_ref, hidden_ref, weight_ref, slab_ref, mine_ref, other_ref, second_ref):
    tile_w, local_ch, lanes = slab_ref.shape
    local_ch //= 3
    block_rows = wide_ref.shape[1]
    images = lanes // block_rows
    edge = edge_ref[...].T
    for x in range(tile_w):
        for n in range(images):
            rows = wide_ref[pl.ds(n * local_ch * tile_w + x, local_ch, stride=tile_w), :]
            before, after = edge_columns(edge, local_ch, n)
            for b in range(3):
                slab_ref[x, b * local_ch : (b + 1) * local_ch, n * block_rows : (n + 1) * block_rows] = tap(
                    rows, b, before[:, x : x + 1], after[:, x : x + 1]
                ).astype(BF16)
    weights = [weight_ref[a] for a in range(3)]
    sums = [None] * 3
    for x in range(1, tile_w - 1):
        total = None
        for a in range(3):
            slab = slab_ref[x + a - 1]
            total = added(total, jnp.dot(weights[a], slab, preferred_element_type=F32))
            sums[a] = added(sums[a], nt(slab, hidden_ref[x]))
        mine_ref[x - 1] = total[:local_ch]
        other_ref[x - 1] = total[local_ch:].astype(BF16)
    for a in range(3):
        second_ref[a] = sums[a]


def added(total, product):
    return product if total is None else total + product


def inner_first_kernel(mine_ref, arrived_ref, hidden_ref, layer_slab, out_ref):
    rows, local_ch, _ = mine_ref.shape
    first = pl.multiple_of(lax.axis_index("chan") * local_ch, local_ch)
    sums = [None] * 3
    for x in range(1, rows + 1):
        grad = masked(mine_ref[x - 1], arrived_ref[x - 1], hidden_ref[x, pl.ds(first, local_ch), :])
        for a in range(3):
            sums[a] = added(sums[a], nt(grad, layer_slab[x + a - 1]))
    for a in range(3):
        out_ref[a] = sums[a]


def masked(mine, arrived, hidden):
    return jnp.where(hidden.astype(F32) > 0, mine + arrived.astype(F32), 0.0).astype(BF16)


def halo_at(own, halo, p):
    return halo[0] if p < 0 else halo[1] if p >= own.shape[0] else own[p]


def outer_kernel(before_ref, after_ref, layer_slab, grad_slab, w_first_ref, w_second_ref,
                 layer_edge, grad_edge, hidden_edge, mine_ref, other_ref):
    tile_w, triple, lanes = layer_slab.shape
    channels = triple // 3
    local_ch = grad_slab.shape[1] // 3
    images = 2
    block_rows = lanes // images
    all_in, all_grad = (images * channels, images * local_ch)
    col = lax.axis_index("col")
    present = (col > 0, col < lax.axis_size("col") - 1)
    for side, (ref, ok) in enumerate(zip((before_ref, after_ref), present)):
        block = jnp.where(ok, ref[...].astype(F32), 0.0)
        corners = block[all_in + all_grad : all_in + all_grad + 8].T
        edge = corners[:, 2:3]
        for n in range(images):
            lanes_here = slice(n * block_rows, (n + 1) * block_rows)
            part = slice(n * channels, (n + 1) * channels)
            rows = block[all_in + n * local_ch : all_in + (n + 1) * local_ch]
            before, after = edge_columns(edge, local_ch, n)
            for b in range(3):
                layer_edge[side, b * channels : (b + 1) * channels, lanes_here] = tap(
                    block[part], b, corners[part, 0:1], corners[part, 1:2]
                ).astype(BF16)
                grad_edge[side, b * local_ch : (b + 1) * local_ch, lanes_here] = tap(
                    rows, b, before, after
                ).astype(BF16)
    first = [w_first_ref[a] for a in range(3)]
    second = [w_second_ref[a] for a in range(3)]
    for side, x in enumerate((0, tile_w - 1)):
        hidden_edge[side] = hidden_row(first, [halo_at(layer_slab, layer_edge, x + a - 1) for a in range(3)])
        total = None
        for a in range(3):
            slab = halo_at(grad_slab, grad_edge, x + a - 1)
            total = added(total, jnp.dot(second[a], slab, preferred_element_type=F32))
        mine_ref[side] = total[:local_ch]
        other_ref[side] = total[local_ch:].astype(BF16)


def second_kernel(wide_ref, inner_ref, grad_slab, grad_edge, hidden_edge, grad_ref, out_ref):
    tile_w = grad_slab.shape[0]
    grad_ref[...] = wide_ref[...].reshape(grad_ref.shape).astype(BF16)
    for a in range(3):
        total = inner_ref[a]
        for side, x in enumerate((0, tile_w - 1)):
            total = total + nt(halo_at(grad_slab, grad_edge, x + a - 1), hidden_edge[side])
        out_ref[a] = total


def last_kernel(mine_ref, arrived_ref, hidden_edge, layer_slab, layer_edge, inner_ref, second_ref, out_ref):
    tile_w = layer_slab.shape[0]
    local_ch = mine_ref.shape[1]
    channels = layer_slab.shape[1] // 3
    first = pl.multiple_of(lax.axis_index("chan") * local_ch, local_ch)
    sums = [inner_ref[a] for a in range(3)]
    for side, x in enumerate((0, tile_w - 1)):
        grad = masked(mine_ref[side], arrived_ref[side], hidden_edge[side, pl.ds(first, local_ch), :])
        for a in range(3):
            sums[a] = sums[a] + nt(grad, halo_at(layer_slab, layer_edge, x + a - 1))
    for a in range(3):
        for b in range(3):
            one = sums[a][:, b * channels : (b + 1) * channels]
            two = second_ref[2 - a, (2 - b) * local_ch : (3 - b) * local_ch, :]
            out_ref[3 * a + b] = jnp.concatenate([one, two], axis=1)


def finish_kernel(factor, own_ref, arrived_ref, first_ref, second_ref):
    local_ch = own_ref.shape[1]
    channels = first_ref.shape[3]
    chan = lax.axis_index("chan")
    for ref, at in ((own_ref, chan), (arrived_ref, 1 - chan)):
        here = pl.ds(pl.multiple_of(at * local_ch, local_ch), local_ch)
        for a in range(3):
            for b in range(3):
                block = ref[3 * a + b] * factor
                first_ref[a, b, here, :] = block[:, :channels]
                second_ref[a, b, here, :] = block[:, channels:]


def swapped(block, axis, step=1):
    return lax.ppermute(block, axis, [(i, i ^ step) for i in range(lax.axis_size(axis))])


def exchanged(partial, axis, *steps):
    rounded = lax.reduce_precision(partial, 8, 7)
    sent = rounded.astype(BF16)
    terms = [rounded] + [swapped(sent, axis, step).astype(F32) for step in steps]
    while len(terms) > 1:
        terms = [sum(terms[i : i + 2]) for i in range(0, len(terms), 2)]
    return terms[0]


def summed(partial):
    peers = lax.axis_size("row")
    step = 1
    while step < peers:
        if step * 2 < peers:
            partial = exchanged(partial, "row", step, 2 * step, 3 * step)
            step *= 4
        else:
            partial = exchanged(partial, "row", step)
            step *= 2
    peers = lax.axis_size("col")
    step = 1
    while step < peers:
        partial = exchanged(partial, "col", step)
        step *= 2
    return partial


def whole(layer_input, features, vol_target, offsets, w_first, w_second):
    images, channels, tile_w, block_rows = layer_input.shape
    local_ch = features.shape[1]
    groups = vol_target.shape[0]
    lanes = images * block_rows
    tile = (tile_w, block_rows)
    plain, framed = ((local_ch + k, *tile) for k in (0, 1))
    swap = lax.axis_size("col") == 2
    routing = routes()
    w_first = w_first.transpose(2, 3, 0, 1)
    w_second = w_second.transpose(2, 3, 0, 1)

    packed = call(functools.partial(pack_kernel, routing), [(framed, BF16)] * len(routing), layer_input, features)
    blocks = []
    for block, route in zip(packed, routing):
        blocks.append(delivered(block, route, 1))

    vol_target, = call(
        fetch_kernel, [(vol_target.shape, BF16)], vol_target, far=True,
        scratch=[pltpu.SemaphoreType.DMA((1,))],
    )

    size = local_ch // groups
    left_grad, own, *outgoing = call(
        functools.partial(correlation_kernel, routing),
        [(plain, BF16), (framed, F32)] + [(framed, BF16)] * len(routing),
        offsets, features, vol_target, *blocks, smem=1, flops=1 << 26,
        scratch=[pltpu.VMEM((DISP, size, *tile), F32), pltpu.VMEM((DISP, *tile), F32)],
    )
    arrivals = []
    for block, route in zip(outgoing, routing):
        arrivals.append(delivered(block, route, -1))

    messages = 1 if swap else 2
    slab_shape, hidden_shape = ((3 * channels, lanes), (channels, lanes))
    lines = (images * channels, block_rows)
    layer_slab, hidden, w_first, w_second, *border = call(
        functools.partial(hidden_kernel, routing),
        [((tile_w, *slab_shape), BF16), ((tile_w, *hidden_shape), BF16),
         ((3, channels, 3 * channels), BF16), ((3, channels, 3 * local_ch), BF16)]
        + [(lines, BF16)] * messages + [(tile, F32)] * messages,
        layer_input, w_first, w_second, *blocks, flops=1 << 28,
        scratch=[pltpu.VMEM((images * channels * tile_w, block_rows), F32), pltpu.VMEM((2, *tile), F32)],
    )
    message = ((images * (channels + local_ch) + 16, block_rows), BF16)
    wide, edge, *sends = call(
        functools.partial(combine_kernel, len(routing)),
        [((images * local_ch * tile_w, block_rows), F32), (tile, F32)] + [message] * messages,
        left_grad, own, *arrivals, *border,
        scratch=[pltpu.VMEM(tile, F32)],
    )
    if swap:
        before = after = swapped(sends[0], "col")
    else:
        before, after = (moved(sends[0], "col", 1), moved(sends[1], "col", -1))
    middle, rim = (tile_w - 2, local_ch, lanes), (2, local_ch, lanes)
    sums = (3, 3 * local_ch, channels)
    grad_slab, mine, other, second = call(
        inner_kernel,
        [((tile_w, 3 * local_ch, lanes), BF16), (middle, F32), (middle, BF16), (sums, F32)],
        wide, edge, hidden, w_second, flops=1 << 28,
    )
    arrived = swapped(other, "chan")
    inner_first, = call(
        inner_first_kernel, [((3, local_ch, 3 * channels), F32)],
        mine, arrived, hidden, layer_slab, flops=1 << 28,
    )
    layer_edge, grad_edge, hidden_edge, mine, other = call(
        outer_kernel,
        [((2, *slab_shape), BF16), ((2, 3 * local_ch, lanes), BF16), ((2, *hidden_shape), BF16),
         (rim, F32), (rim, BF16)],
        before, after, layer_slab, grad_slab, w_first, w_second, flops=1 << 27,
    )
    arrived = swapped(other, "chan")
    grad_features, second = call(
        second_kernel, [((images, *plain), BF16), (sums, F32)],
        wide, second, grad_slab, grad_edge, hidden_edge, flops=1 << 27,
    )
    partial, = call(
        last_kernel, [((9, local_ch, 2 * channels), F32)],
        mine, arrived, hidden_edge, layer_slab, layer_edge, inner_first, second, flops=1 << 27,
    )
    total = summed(partial)
    factor = 1.0 / math.sqrt(
        2.0 * tile_w * lax.axis_size("col") * block_rows * lax.axis_size("row")
    )
    first, second = call(
        functools.partial(finish_kernel, factor), [((3, 3, channels, channels), F32)] * 2,
        total, swapped(total, "chan"),
    )
    return (grad_features, first.transpose(2, 3, 0, 1), second.transpose(2, 3, 0, 1))


def solution(mesh):
    return jax.shard_map(
        whole,
        mesh=mesh,
        in_specs=(
            P(None, None, ("groups", "col"), "row"),
            P(None, "chan", ("groups", "col"), "row"),
            P("chan", None, ("groups", "col"), "row"),
            P("row", ("groups", "col")),
            P(),
            P(),
        ),
        out_specs=(
            P(None, "chan", ("groups", "col"), "row"),
            P("groups", None, None, None),
            P("groups", None, None, None),
        ),
        check_vma=False,
    )
```

```python
import functools
import math

import jax
import jax.numpy as jnp
from jax import lax
from jax.experimental import pallas as pl
from jax.experimental.pallas import tpu as pltpu
from jax.sharding import PartitionSpec as P


DISP = 40
MAXOFF = 2
F32 = jnp.float32
BF16 = jnp.bfloat16
SPACE = 12 << 20


def call(kernel, outs, *args, smem=0, far=False, last=0, scratch=(), flops=1 << 20):
    whole = pl.BlockSpec(memory_space=pltpu.VMEM)
    given = pl.BlockSpec(memory_space=pltpu.HBM) if far else whole
    if last:
        away = pl.BlockSpec(memory_space=pltpu.HBM)
        count = len(args) - len(outs) if last > 1 else len(args)
        return pl.pallas_call(
            kernel,
            in_specs=[whole] * count + [away] * (len(args) - count),
            out_specs=[away] * len(outs),
            out_shape=[jax.ShapeDtypeStruct(s, t) for s, t in outs],
            input_output_aliases={count + i: i for i in range(len(args) - count)},
            scratch_shapes=list(scratch),
            compiler_params=pltpu.CompilerParams(vmem_limit_bytes=SPACE),
        )(*args)
    return pl.pallas_call(
        kernel,
        in_specs=[pl.BlockSpec(memory_space=pltpu.SMEM)] * smem + [given] * (len(args) - smem),
        out_specs=[whole] * len(outs),
        out_shape=[jax.ShapeDtypeStruct(s, t) for s, t in outs],
        scratch_shapes=list(scratch),
        compiler_params=pltpu.CompilerParams(vmem_limit_bytes=SPACE),
        cost_estimate=pl.CostEstimate(flops=flops, bytes_accessed=1 << 20, transcendentals=0),
    )(*args)


def routes():
    peers = lax.axis_size("row")
    if peers == MAXOFF + 2 and peers & (peers - 1) == 0:
        return [("swap", mask) for mask in range(1, peers)]
    return [("line", k) for k in (*range(1, MAXOFF + 2), -1)]


def distance(route):
    kind, value = route
    if kind == "line":
        return value
    row = lax.axis_index("row")
    return row - (row ^ value)


def has_edges(route):
    kind, value = route
    if kind == "line":
        return abs(value) == 1
    return any(abs(i - (i ^ value)) == 1 for i in range(lax.axis_size("row")))


def delivered(block, route, sign):
    kind, value = route
    if kind == "swap":
        return swapped(block, "row", value)
    return moved(block, "row", sign * value)


def moved(block, axis, distance):
    peers = lax.axis_size(axis)
    return lax.ppermute(block, axis, [(i - distance, i) for i in range(peers) if 0 <= i - distance < peers])


def tap(rows, b, before, after):
    if b == 1:
        return rows
    lane = lax.broadcasted_iota(jnp.int32, rows.shape, 1)
    last = rows.shape[1] - 1
    if b == 0:
        return jnp.where(lane == 0, jnp.broadcast_to(before, rows.shape), pltpu.roll(rows, 1, 1))
    return jnp.where(lane == last, jnp.broadcast_to(after, rows.shape), pltpu.roll(rows, last, 1))


def nt(a, b):
    return lax.dot_general(a, b, (((1,), (1,)), ((), ())), preferred_element_type=F32)


def fetch_kernel(*refs):
    count = len(refs) // 2
    sources, targets, sems = refs[:count], refs[count:-1], refs[-1]
    copies = [pltpu.make_async_copy(s, t, sems.at[i]) for i, (s, t) in enumerate(zip(sources, targets))]
    for copy in copies:
        copy.start()
    for copy in copies:
        copy.wait()


def pack_kernel(routing, layer_ref, right_ref, *out_refs):
    images, channels, tile_w, block_rows = layer_ref.shape
    local_ch = right_ref.shape[0]
    shape = (tile_w, block_rows)
    lane = lax.broadcasted_iota(jnp.int32, shape, 1)
    first = jnp.zeros(shape, F32)
    last = jnp.zeros(shape, F32)
    for n in range(images):
        for c in range(channels):
            tile = layer_ref[n, c].astype(F32)
            here = lane == n * channels + c
            first = jnp.where(here, jnp.broadcast_to(tile[:, :1], shape), first)
            last = jnp.where(here, jnp.broadcast_to(tile[:, block_rows - 1 :], shape), last)
    for route, out_ref in zip(routing, out_refs):
        ahead = distance(route) if route[0] == "line" else -distance(route)
        out_ref[:local_ch] = right_ref[...]
        out_ref[local_ch] = jnp.where(ahead == 1, last, jnp.where(ahead == -1, first, 0.0)).astype(BF16)


def correlation_kernel(routing, offset_ref, features_ref, target_ref, *rest):
    count = len(routing)
    block_refs, (left_out, own_out) = rest[:count], rest[count : count + 2]
    out_refs, (moved_ref, residual_ref) = rest[count + 2 : -2], rest[-2:]
    ahead = [distance(route) for route in routing]
    offset = offset_ref[0, 0]
    local_ch, tile_w, block_rows = features_ref.shape[1:]
    groups = target_ref.shape[0]
    size = local_ch // groups
    inv_size = 1.0 / size
    shape = (tile_w, block_rows)
    lane = lax.broadcasted_iota(jnp.int32, shape, 1)
    zero = jnp.zeros(shape, F32)

    def column(tile, at, kind, c, into):
        picked = jnp.broadcast_to(tile[:, at : at + 1], shape)
        return jnp.where(lane == kind * local_ch + c, picked, into)

    def one_group(g, edges):
        end_main, end_spill, start_main, end_left, start_left = edges
        base = g * size

        def scaled_left(c):
            return features_ref[0, base + c].astype(F32) * inv_size

        left, main, spill = [], [], []
        for c in range(size):
            here = features_ref[1, base + c].astype(F32)
            before = zero
            for k, block_ref in zip(ahead, block_refs):
                block = block_ref[base + c].astype(F32)
                here = jnp.where(k == offset, block, here)
                before = jnp.where(k == offset + 1, block, before)
            left.append(scaled_left(c))
            main.append(here)
            spill.append(before)
        for d in range(DISP):
            products = []
            for c in range(size):
                moved = main[c]
                if d:
                    moved = pltpu.roll(jnp.where(lane >= block_rows - d, spill[c], moved), d, 1)
                moved_ref[d, c] = moved
                products.append(left[c] * moved)
            while len(products) > 1:
                products = [sum(products[i : i + 2]) for i in range(0, len(products), 2)]
            residual_ref[d] = products[0] - target_ref[g, d].astype(F32)
        for first in range(0, size, 8):
            channels = range(first, min(first + 8, size))
            left_grad = {c: zero for c in channels}
            whole_grad = {c: zero for c in channels}
            spill_grad = {c: zero for c in channels}
            scaled = {c: scaled_left(c) for c in channels}
            for d in range(DISP):
                residual = residual_ref[d]
                for c in channels:
                    left_grad[c] = left_grad[c] + residual * moved_ref[d, c]
                    part = residual * scaled[c]
                    if d:
                        part = pltpu.roll(part, block_rows - d, 1)
                        spill_grad[c] = spill_grad[c] + jnp.where(lane >= block_rows - d, part, 0.0)
                    whole_grad[c] = whole_grad[c] + part
            for c in channels:
                ch = base + c
                main_grad = whole_grad[c] - spill_grad[c]
                final = (left_grad[c] * inv_size).astype(BF16)
                left_out[ch] = final
                final = final.astype(F32)
                own_out[ch] = jnp.where(offset == 0, main_grad, 0.0)
                for k, out_ref in zip(ahead, out_refs):
                    out_ref[ch] = jnp.where(
                        offset + 1 == k, spill_grad[c], jnp.where(offset == k, main_grad, 0.0)
                    ).astype(BF16)
                end_main = column(main_grad, block_rows - 1, 0, ch, end_main)
                end_spill = column(spill_grad[c], block_rows - 1, 0, ch, end_spill)
                start_main = column(main_grad, 0, 1, ch, start_main)
                end_left = column(final, block_rows - 1, 2, ch, end_left)
                start_left = column(final, 0, 3, ch, start_left)
        return end_main, end_spill, start_main, end_left, start_left

    end_main, end_spill, start_main, end_left, start_left = lax.fori_loop(
        0, groups, one_group, (zero,) * 5
    )

    def edges(k):
        tile = jnp.where(offset == k + 1, end_main, 0.0) + jnp.where(offset == k, end_spill, 0.0)
        tile = tile + jnp.where(offset == k - 1, start_main, 0.0)
        return tile + jnp.where(k == -1, end_left, jnp.where(k == 1, start_left, 0.0))

    own_out[local_ch] = edges(0)
    for k, out_ref in zip(ahead, out_refs):
        out_ref[local_ch] = edges(k).astype(BF16)


def hidden_kernel(routing, layer_ref, first_ref, second_ref, *rest):
    block_refs, (slab_ref, hidden_ref, first_out, second_out) = rest[: len(routing)], rest[len(routing) :][:4]
    rest = rest[len(routing) + 4 :]
    rows_refs, corner_refs, (wide_ref, small_ref) = rest[: len(rest) // 2 - 1], rest[len(rest) // 2 - 1 : -2], rest[-2:]
    images, channels, tile_w, block_rows = layer_ref.shape
    wide_ref[...] = layer_ref[...].astype(F32).reshape(wide_ref.shape)
    before = after = jnp.zeros((tile_w, block_rows), F32)
    for route, block_ref in zip(routing, block_refs):
        k = distance(route)
        tile = block_ref[block_ref.shape[0] - 1].astype(F32)
        before = jnp.where(k == 1, tile, before)
        after = jnp.where(k == -1, tile, after)
    small_ref[0] = before
    small_ref[1] = after
    before, after = before.T, after.T
    for x in range(tile_w):
        for n in range(images):
            rows = wide_ref[pl.ds(n * channels * tile_w + x, channels, stride=tile_w), :]
            part = slice(n * channels, (n + 1) * channels)
            for b in range(3):
                slab_ref[x, b * channels : (b + 1) * channels, n * block_rows : (n + 1) * block_rows] = tap(
                    rows, b, before[part, x : x + 1], after[part, x : x + 1]
                ).astype(BF16)
    weights = first_weights(first_ref)
    local_ch = channels // lax.axis_size("chan")
    for a, (w, v) in enumerate(zip(weights, second_weights(second_ref, lax.axis_index("chan"), local_ch))):
        first_out[a] = w
        second_out[a] = v
    for x in range(1, tile_w - 1):
        hidden_ref[x] = hidden_row(weights, [slab_ref[x + a - 1] for a in range(3)])
    for x, rows_ref, corner_ref in zip(border_rows(len(rows_refs), tile_w), rows_refs, corner_refs):
        rows_ref[...] = wide_ref[pl.ds(x, images * channels, stride=tile_w), :].astype(BF16)
        corner_ref[...] = stacked_lines([small_ref[j, pl.ds(x, 1), :] for j in range(2)], tile_w)


def border_rows(messages, tile_w):
    if messages == 1:
        return [jnp.where(lax.axis_index("col") == 0, tile_w - 1, 0)]
    return [tile_w - 1, 0]


def stacked_lines(lines, height):
    shape = (height, lines[0].shape[1])
    sub = lax.broadcasted_iota(jnp.int32, shape, 0)
    tile = jnp.zeros(shape, F32)
    for j, line in enumerate(lines):
        tile = jnp.where(sub == j, jnp.broadcast_to(line, shape), tile)
    return tile


def first_weights(weight_ref):
    return [jnp.concatenate([weight_ref[a, b] for b in range(3)], axis=1) for a in range(3)]


def hidden_row(weights, slabs):
    total = None
    for w, s in zip(weights, slabs):
        product = jnp.dot(w, s, preferred_element_type=F32)
        total = product if total is None else total + product
    return jnp.maximum(total, 0.0).astype(BF16)


def combine_kernel(arrivals, left_ref, own_ref, *rest):
    block_refs, rest = rest[:arrivals], rest[arrivals:]
    count = (len(rest) - 3) // 3
    rows_refs, corner_refs = rest[:count], rest[count : 2 * count]
    wide_ref, edge_ref = rest[2 * count : 2 * count + 2]
    sends, small_ref = rest[2 * count + 2 : -1], rest[-1]
    local_ch, tile_w, block_rows = left_ref.shape
    images = wide_ref.shape[0] // (local_ch * tile_w)
    rows = local_ch * tile_w
    shape = (rows, block_rows)
    lane = lax.broadcasted_iota(jnp.int32, (tile_w, block_rows), 1)
    left = left_ref[...]
    total = own_ref[...]
    for block_ref in block_refs:
        total = total + block_ref[...].astype(F32)
    right, edge = total[:local_ch].astype(BF16), total[local_ch]
    wide_ref[:rows] = left.astype(F32).reshape(shape)
    wide_ref[rows:] = right.astype(F32).reshape(shape)
    outside = lane < jnp.where(lax.axis_index("row") == 0, local_ch, 0)
    edge = jnp.where(outside, 0.0, edge)
    edge_ref[...] = edge
    small_ref[...] = edge
    all_in, all_grad = (rows_refs[0].shape[0], images * local_ch)
    for x, rows_ref, corner_ref, send_ref in zip(border_rows(count, tile_w), rows_refs, corner_refs, sends):
        send_ref[:all_in] = rows_ref[...]
        send_ref[all_in : all_in + all_grad] = wide_ref[pl.ds(x, all_grad, stride=tile_w), :].astype(BF16)
        lines = [corner_ref[0:1, :], corner_ref[1:2, :], small_ref[pl.ds(x, 1), :]]
        send_ref[all_in + all_grad :] = stacked_lines(lines, send_ref.shape[0] - all_in - all_grad).astype(BF16)


def second_weights(weight_ref, chan, local_ch):
    first = pl.multiple_of(chan * local_ch, local_ch)
    result = []
    for a in range(3):
        parts = []
        for b in range(3):
            w = weight_ref[2 - a, 2 - b, pl.ds(first, local_ch), :].astype(F32)
            half = w.shape[1] // 2
            parts.append(jnp.where(chan == 0, w, jnp.concatenate([w[:, half:], w[:, :half]], axis=1)))
        result.append(jnp.concatenate(parts, axis=0).T.astype(BF16))
    return result


def edge_columns(edge, local_ch, n):
    at = (2, 3) if n == 0 else (0, 1)
    return tuple(edge[k * local_ch : (k + 1) * local_ch] for k in at)


def inner_kernel(wide_ref, edge_ref, hidden_ref, weight_ref, slab_ref, mine_ref, other_ref, second_ref):
    tile_w, local_ch, lanes = slab_ref.shape
    local_ch //= 3
    block_rows = wide_ref.shape[1]
    images = lanes // block_rows
    edge = edge_ref[...].T
    for x in range(tile_w):
        for n in range(images):
            rows = wide_ref[pl.ds(n * local_ch * tile_w + x, local_ch, stride=tile_w), :]
            before, after = edge_columns(edge, local_ch, n)
            for b in range(3):
                slab_ref[x, b * local_ch : (b + 1) * local_ch, n * block_rows : (n + 1) * block_rows] = tap(
                    rows, b, before[:, x : x + 1], after[:, x : x + 1]
                ).astype(BF16)
    weights = [weight_ref[a] for a in range(3)]
    sums = [None] * 3
    for x in range(1, tile_w - 1):
        total = None
        for a in range(3):
            slab = slab_ref[x + a - 1]
            total = added(total, jnp.dot(weights[a], slab, preferred_element_type=F32))
            sums[a] = added(sums[a], nt(slab, hidden_ref[x]))
        mine_ref[x - 1] = total[:local_ch]
        other_ref[x - 1] = total[local_ch:].astype(BF16)
    for a in range(3):
        second_ref[a] = sums[a]


def added(total, product):
    return product if total is None else total + product


def inner_first_kernel(mine_ref, arrived_ref, hidden_ref, layer_slab, out_ref):
    rows, local_ch, _ = mine_ref.shape
    first = pl.multiple_of(lax.axis_index("chan") * local_ch, local_ch)
    sums = [None] * 3
    for x in range(1, rows + 1):
        grad = masked(mine_ref[x - 1], arrived_ref[x - 1], hidden_ref[x, pl.ds(first, local_ch), :])
        for a in range(3):
            sums[a] = added(sums[a], nt(grad, layer_slab[x + a - 1]))
    for a in range(3):
        out_ref[a] = sums[a]


def masked(mine, arrived, hidden):
    return jnp.where(hidden.astype(F32) > 0, mine + arrived.astype(F32), 0.0).astype(BF16)


def halo_at(own, halo, p):
    return halo[0] if p < 0 else halo[1] if p >= own.shape[0] else own[p]


def outer_kernel(before_ref, after_ref, layer_slab, grad_slab, w_first_ref, w_second_ref,
                 layer_edge, grad_edge, hidden_edge, mine_ref, other_ref):
    tile_w, triple, lanes = layer_slab.shape
    channels = triple // 3
    local_ch = grad_slab.shape[1] // 3
    images = 2
    block_rows = lanes // images
    all_in, all_grad = (images * channels, images * local_ch)
    col = lax.axis_index("col")
    present = (col > 0, col < lax.axis_size("col") - 1)
    for side, (ref, ok) in enumerate(zip((before_ref, after_ref), present)):
        block = jnp.where(ok, ref[...].astype(F32), 0.0)
        corners = block[all_in + all_grad : all_in + all_grad + 8].T
        edge = corners[:, 2:3]
        for n in range(images):
            lanes_here = slice(n * block_rows, (n + 1) * block_rows)
            part = slice(n * channels, (n + 1) * channels)
            rows = block[all_in + n * local_ch : all_in + (n + 1) * local_ch]
            before, after = edge_columns(edge, local_ch, n)
            for b in range(3):
                layer_edge[side, b * channels : (b + 1) * channels, lanes_here] = tap(
                    block[part], b, corners[part, 0:1], corners[part, 1:2]
                ).astype(BF16)
                grad_edge[side, b * local_ch : (b + 1) * local_ch, lanes_here] = tap(
                    rows, b, before, after
                ).astype(BF16)
    first = [w_first_ref[a] for a in range(3)]
    second = [w_second_ref[a] for a in range(3)]
    for side, x in enumerate((0, tile_w - 1)):
        hidden_edge[side] = hidden_row(first, [halo_at(layer_slab, layer_edge, x + a - 1) for a in range(3)])
        total = None
        for a in range(3):
            slab = halo_at(grad_slab, grad_edge, x + a - 1)
            total = added(total, jnp.dot(second[a], slab, preferred_element_type=F32))
        mine_ref[side] = total[:local_ch]
        other_ref[side] = total[local_ch:].astype(BF16)


def second_kernel(wide_ref, inner_ref, grad_slab, grad_edge, hidden_edge, grad_ref, out_ref):
    tile_w = grad_slab.shape[0]
    grad_ref[...] = wide_ref[...].reshape(grad_ref.shape).astype(BF16)
    for a in range(3):
        total = inner_ref[a]
        for side, x in enumerate((0, tile_w - 1)):
            total = total + nt(halo_at(grad_slab, grad_edge, x + a - 1), hidden_edge[side])
        out_ref[a] = total


def last_kernel(mine_ref, arrived_ref, hidden_edge, layer_slab, layer_edge, inner_ref, second_ref, out_ref):
    tile_w = layer_slab.shape[0]
    local_ch = mine_ref.shape[1]
    channels = layer_slab.shape[1] // 3
    first = pl.multiple_of(lax.axis_index("chan") * local_ch, local_ch)
    sums = [inner_ref[a] for a in range(3)]
    for side, x in enumerate((0, tile_w - 1)):
        grad = masked(mine_ref[side], arrived_ref[side], hidden_edge[side, pl.ds(first, local_ch), :])
        for a in range(3):
            sums[a] = sums[a] + nt(grad, halo_at(layer_slab, layer_edge, x + a - 1))
    for a in range(3):
        for b in range(3):
            one = sums[a][:, b * channels : (b + 1) * channels]
            two = second_ref[2 - a, (2 - b) * local_ch : (3 - b) * local_ch, :]
            out_ref[3 * a + b] = jnp.concatenate([one, two], axis=1)


def finish_kernel(factor, mine, sum_ref, *rest):
    first_out, second_out, first_ref, second_ref, sems = rest[-5:]
    local_ch = sum_ref.shape[1]
    channels = first_ref.shape[3]
    chan = lax.axis_index("chan")
    here = pl.ds(pl.multiple_of((chan if mine else 1 - chan) * local_ch, local_ch), local_ch)
    copies = []
    for a in range(3):
        for b in range(3):
            block = sum_ref[3 * a + b] * factor
            first_ref[a, b] = block[:, :channels]
            second_ref[a, b] = block[:, channels:]
        copies.append(pltpu.make_async_copy(first_ref.at[a], first_out.at[a, :, here, :], sems.at[0, a]))
        copies.append(pltpu.make_async_copy(second_ref.at[a], second_out.at[a, :, here, :], sems.at[1, a]))
        copies[-2].start()
        copies[-1].start()
    for copy in copies:
        copy.wait()


def swapped(block, axis, step=1):
    return lax.ppermute(block, axis, [(i, i ^ step) for i in range(lax.axis_size(axis))])


def exchanged(partial, axis, *steps):
    rounded = lax.reduce_precision(partial, 8, 7)
    sent = rounded.astype(BF16)
    terms = [rounded]
    for step in steps:
        terms.append(swapped(sent, axis, step).astype(F32))
    while len(terms) > 1:
        terms = [sum(terms[i : i + 2]) for i in range(0, len(terms), 2)]
    return terms[0]


def summed(partial):
    peers = lax.axis_size("col")
    step = 1
    while step < peers:
        partial = exchanged(partial, "col", step)
        step *= 2
    peers = lax.axis_size("row")
    step = 1
    while step < peers:
        if step * 2 < peers:
            partial = exchanged(partial, "row", step, 2 * step, 3 * step)
            step *= 4
        else:
            partial = exchanged(partial, "row", step)
            step *= 2
    return partial


def whole(layer_input, features, vol_target, offsets, w_first, w_second):
    images, channels, tile_w, block_rows = layer_input.shape
    local_ch = features.shape[1]
    groups = vol_target.shape[0]
    lanes = images * block_rows
    tile = (tile_w, block_rows)
    plain, framed = ((local_ch + k, *tile) for k in (0, 1))
    swap = lax.axis_size("col") == 2
    routing = routes()
    w_first = w_first.transpose(2, 3, 0, 1)
    w_second = w_second.transpose(2, 3, 0, 1)

    edged = [route for route in routing if has_edges(route)]
    right = features[1]
    packed = call(functools.partial(pack_kernel, edged), [(framed, BF16)] * len(edged), layer_input, right)
    blocks = []
    for route in routing:
        blocks.append(delivered(packed[edged.index(route)] if route in edged else right, route, 1))

    vol_target, = call(
        fetch_kernel, [(vol_target.shape, BF16)], vol_target, far=True,
        scratch=[pltpu.SemaphoreType.DMA((1,))],
    )

    size = local_ch // groups
    left_grad, own, *outgoing = call(
        functools.partial(correlation_kernel, routing),
        [(plain, BF16), (framed, F32)] + [(framed, BF16)] * len(routing),
        offsets, features, vol_target, *blocks, smem=1, flops=1 << 26,
        scratch=[pltpu.VMEM((DISP, size, *tile), F32), pltpu.VMEM((DISP, *tile), F32)],
    )
    arrivals = []
    for block, route in zip(outgoing, routing):
        arrivals.append(delivered(block, route, -1))

    messages = 1 if swap else 2
    slab_shape, hidden_shape = ((3 * channels, lanes), (channels, lanes))
    lines = (images * channels, block_rows)
    layer_slab, hidden, w_first, w_second, *border = call(
        functools.partial(hidden_kernel, routing),
        [((tile_w, *slab_shape), BF16), ((tile_w, *hidden_shape), BF16),
         ((3, channels, 3 * channels), BF16), ((3, channels, 3 * local_ch), BF16)]
        + [(lines, BF16)] * messages + [(tile, F32)] * messages,
        layer_input, w_first, w_second, *blocks, flops=1 << 28,
        scratch=[pltpu.VMEM((images * channels * tile_w, block_rows), F32), pltpu.VMEM((2, *tile), F32)],
    )
    message = ((images * (channels + local_ch) + 16, block_rows), BF16)
    wide, edge, *sends = call(
        functools.partial(combine_kernel, len(routing)),
        [((images * local_ch * tile_w, block_rows), F32), (tile, F32)] + [message] * messages,
        left_grad, own, *arrivals, *border,
        scratch=[pltpu.VMEM(tile, F32)],
    )
    if swap:
        before = after = swapped(sends[0], "col")
    else:
        before, after = (moved(sends[0], "col", 1), moved(sends[1], "col", -1))
    middle, rim = (tile_w - 2, local_ch, lanes), (2, local_ch, lanes)
    sums = (3, 3 * local_ch, channels)
    grad_slab, mine, other, second = call(
        inner_kernel,
        [((tile_w, 3 * local_ch, lanes), BF16), (middle, F32), (middle, BF16), (sums, F32)],
        wide, edge, hidden, w_second, flops=1 << 28,
    )
    arrived = swapped(other, "chan")
    inner_first, = call(
        inner_first_kernel, [((3, local_ch, 3 * channels), F32)],
        mine, arrived, hidden, layer_slab, flops=1 << 28,
    )
    layer_edge, grad_edge, hidden_edge, mine, other = call(
        outer_kernel,
        [((2, *slab_shape), BF16), ((2, 3 * local_ch, lanes), BF16), ((2, *hidden_shape), BF16),
         (rim, F32), (rim, BF16)],
        before, after, layer_slab, grad_slab, w_first, w_second, flops=1 << 27,
    )
    arrived = swapped(other, "chan")
    grad_features, second = call(
        second_kernel, [((images, *plain), BF16), (sums, F32)],
        wide, second, grad_slab, grad_edge, hidden_edge, flops=1 << 27,
    )
    partial, = call(
        last_kernel, [((9, local_ch, 2 * channels), F32)],
        mine, arrived, hidden_edge, layer_slab, layer_edge, inner_first, second, flops=1 << 27,
    )
    total = summed(partial)
    factor = 1.0 / math.sqrt(
        2.0 * tile_w * lax.axis_size("col") * block_rows * lax.axis_size("row")
    )
    others = swapped(total, "chan")
    kernels = [((3, 3, channels, channels), F32)] * 2
    room = [pltpu.VMEM((3, 3, local_ch, channels), F32)] * 2 + [pltpu.SemaphoreType.DMA((2, 3))]
    halves = call(functools.partial(finish_kernel, factor, True), kernels, total, last=1, scratch=room)
    first, second = call(
        functools.partial(finish_kernel, factor, False), kernels, others, *halves, last=2, scratch=room
    )
    return (grad_features, first.transpose(2, 3, 0, 1), second.transpose(2, 3, 0, 1))


def solution(mesh):
    return jax.shard_map(
        whole,
        mesh=mesh,
        in_specs=(
            P(None, None, ("groups", "col"), "row"),
            P(None, "chan", ("groups", "col"), "row"),
            P("chan", None, ("groups", "col"), "row"),
            P("row", ("groups", "col")),
            P(),
            P(),
        ),
        out_specs=(
            P(None, "chan", ("groups", "col"), "row"),
            P("groups", None, None, None),
            P("groups", None, None, None),
        ),
        check_vma=False,
    )
```
